256 devices in a mesh: tm: 32 (over y, z), dom: 8 (over x, core).
Axes of the slice: x: 4, y: 4, z: 8, core: 2. Of those that a mesh axis runs over, the one named last changes fastest.
Arguments:
- iterates: float32 [64, 2, 4096, 256], P('tm', None, 'dom'), may hold values from -6 to 6
- noise_draws: bfloat16 [64, 2, 4096, 256], P('tm', None, 'dom'), may hold values from -6 to 6
- drift_scale: float32 [64], P('tm'), may hold values from 0.05 to 0.2
- noise_scale: float32 [64], P('tm'), may hold values from 0.05 to 0.2
- step_embed: float32 [64, 256], P('tm'), may hold values from -3 to 3
- self_weight: bfloat16 [2, 256, 256], replicated, may hold values from -0.375 to 0.375
- neighbor_weight: bfloat16 [2, 256, 256], replicated, may hold values from -0.375 to 0.375
- output_weight: bfloat16 [2, 256, 256], replicated, may hold values from -0.375 to 0.375
- drift_weight: bfloat16 [256, 256], replicated, may hold values from -0.375 to 0.375
- local_columns: int32 [32, 4], P('dom'), may hold values from 0 to 3
- tile_values: bfloat16 [32, 4, 128, 128], P('dom'), may hold values from -0.25 to 0.25
- send_blocks: int32 [8, 2, 2], P('dom'), may hold values from 0 to 3
- receive_rows: int32 [8, 2, 2], P('dom'), may hold values from 0 to 3
- remote_values: bfloat16 [8, 2, 2, 128, 128], P('dom'), may hold values from -0.5 to 0.5
Outputs:
- next_iterates: float32 [64, 2, 4096, 256], P('tm', None, 'dom')
The draws below stay inside these ranges and needn't reach their ends.
Inputs may be any that keep to these rules, and one draw needn't show every extreme that they name: `local_columns`: column block within the tile's own partition. In round r partition p sends its blocks send_blocks[p, r, :] to partition p XOR 2**r. `receive_rows`: row block within the receiving partition.
All inputs are finite; a program needn't handle non-finite values.
Results may differ from the reference program's by a relative error of at most 0.006.
Values may be sent and summed in bfloat16 or wider, within the bound.
No kernel may reach another device: no remote copies, remote signals or barrier semaphores. Data moves between devices by JAX's collectives and lax.ppermute only.
A program may use at most 128 MiB of HBM per device.

```python
import math
import jax
import jax.numpy as jnp
import numpy as np
from jax import lax

D = 256
BS = 128
TPR = 4
SENT = 2
ROUNDS = 2
LAYERS = 2
SHOWERS = 2
CELL_DEV = 512
STEPS = 64
CELLS = 4096
BLOCK_DEV = 4
N_DOM = 8


def place_ends(values, own_key, low, largest):
    index_at = [jax.random.randint(jax.random.fold_in(own_key, axis), (), 0, length) for axis, length in enumerate(values.shape)]
    main_axis = values.shape.index(max(values.shape))
    beside = index_at[:main_axis] + [(index_at[main_axis] + 1) % values.shape[main_axis]] + index_at[main_axis + 1:]
    return values.at[tuple(index_at)].set(low).at[tuple(beside)].set(largest)


def steps_of(key, dims, shards, least, high):
    gain, own = 1.0, jax.random.fold_in(key, 6)
    for axis_at, parts in shards:
        heights = jnp.exp(jax.random.uniform(jax.random.fold_in(own, axis_at), (parts,), jnp.float32, least / len(shards), high / len(shards)))
        gain = gain * jnp.repeat(heights, dims[axis_at] // parts).reshape([-1 if axis == axis_at else 1 for axis in range(len(dims))])
    return gain


def centred(key, dims, width, limit, pieces=(), dtype=jnp.bfloat16):
    entries = jax.random.normal(key, dims, jnp.float32) * width
    if len(pieces) > 0:
        entries = steps_of(key, dims, pieces, -0.22, 0.18) * entries
    return jnp.clip(entries, min=-limit, max=limit).astype(dtype)


def setup_inputs(seed: int = 0) -> dict:
    streams_of = jax.random.split(jax.random.key(seed), 15)
    iterates = centred(streams_of[0], (STEPS, SHOWERS, CELLS, D), 1.0, 6.0, ((0, 32), (2, 8)), jnp.float32)
    noise_draws = centred(streams_of[1], (STEPS, SHOWERS, CELLS, D), 1.0, 6.0, ((0, 32), (2, 8)))
    drift_scale = jnp.clip(jnp.exp(math.log(0.2) - 1.3862944 * jax.random.uniform(streams_of[2], (STEPS,), jnp.float32) ** steps_of(streams_of[2], (STEPS,), ((0, 32),), -0.2, 0.2)), 0.05, 0.2)
    noise_scale = jnp.clip(jnp.exp(math.log(0.2) - 1.3862944 * jax.random.uniform(streams_of[3], (STEPS,), jnp.float32) ** steps_of(streams_of[3], (STEPS,), ((0, 32),), -0.2, 0.2)), 0.05, 0.2)
    step_embed = centred(streams_of[4], (STEPS, D), 0.5, 3.0, ((0, 32),), jnp.float32)
    self_weight = centred(streams_of[5], (LAYERS, D, D), D ** -0.5, 0.375)
    neighbor_weight = centred(streams_of[6], (LAYERS, D, D), D ** -0.5, 0.375)
    output_weight = centred(streams_of[7], (LAYERS, D, D), D ** -0.5, 0.375)
    drift_weight = centred(streams_of[8], (D, D), D ** -0.5, 0.375)
    local_columns = place_ends(jax.random.randint(streams_of[9], (CELLS // BS, TPR), 0, BLOCK_DEV), jax.random.fold_in(streams_of[9], 1), 0, BLOCK_DEV - 1).astype(jnp.int32)
    tile_values = centred(streams_of[10], (CELLS // BS, TPR, BS, BS), (TPR * BS) ** -0.5, 0.25, ((0, 8),))
    send_blocks = place_ends(jax.random.randint(streams_of[11], (N_DOM, ROUNDS, SENT), 0, BLOCK_DEV), jax.random.fold_in(streams_of[11], 1), 0, BLOCK_DEV - 1).astype(jnp.int32)
    receive_rows = place_ends(jax.random.randint(streams_of[12], (N_DOM, ROUNDS, SENT), 0, BLOCK_DEV), jax.random.fold_in(streams_of[12], 1), 0, BLOCK_DEV - 1).astype(jnp.int32)
    remote_values = centred(streams_of[13], (N_DOM, ROUNDS, SENT, BS, BS), BS ** -0.5, 0.5, ((0, 8),))
    return {"iterates": iterates, "noise_draws": noise_draws, "drift_scale": drift_scale, "noise_scale": noise_scale, "step_embed": step_embed, "self_weight": self_weight, "neighbor_weight": neighbor_weight, "output_weight": output_weight, "drift_weight": drift_weight, "local_columns": local_columns, "tile_values": tile_values, "send_blocks": send_blocks, "receive_rows": receive_rows, "remote_values": remote_values}


def reference(iterates, noise_draws, drift_scale, noise_scale, step_embed, self_weight, neighbor_weight, output_weight, drift_weight, local_columns, tile_values, send_blocks, receive_rows, remote_values):
    block_count = CELLS // BS
    per_part = CELL_DEV // BS
    block_base = (jnp.arange(block_count) // per_part * per_part).astype(jnp.int32)
    global_columns = block_base[:, None] + local_columns
    partition = np.arange(N_DOM)[:, None]
    round_index = np.arange(ROUNDS)[None, :]
    partner = partition ^ (1 << round_index)
    source_blocks = (partner[:, :, None] * per_part + send_blocks[partner, round_index]).astype(jnp.int32)
    target_blocks = (partition[:, :, None] * per_part + receive_rows).astype(jnp.int32)
    tiles_wide = tile_values.astype(jnp.float32)
    remote_wide = remote_values.astype(jnp.float32)

    def drift_of(iterate, embed):
        hidden = iterate.astype(jnp.bfloat16)
        for layer in range(LAYERS):
            blocked = hidden.reshape(SHOWERS, block_count, BS, D).astype(jnp.float32)
            columns = blocked[:, global_columns]
            summed = jnp.einsum('rjab,srjbd->srad', tiles_wide, columns)
            remote_terms = jnp.einsum('prkab,sprkbd->sprkad', remote_wide, blocked[:, source_blocks])
            summed = summed.at[:, target_blocks.reshape(-1)].add(remote_terms.reshape(SHOWERS, -1, BS, D))
            mixed = summed.reshape(SHOWERS, CELLS, D).astype(jnp.bfloat16)
            preact = jnp.dot(hidden, self_weight[layer], preferred_element_type=jnp.float32)
            preact = preact + jnp.dot(mixed, neighbor_weight[layer], preferred_element_type=jnp.float32) + embed
            activated = jax.nn.silu(preact).astype(jnp.bfloat16)
            hidden = (hidden.astype(jnp.float32) + jnp.dot(activated, output_weight[layer], preferred_element_type=jnp.float32)).astype(jnp.bfloat16)
        return jnp.dot(hidden, drift_weight, preferred_element_type=jnp.float32)

    def advance(running, inputs):
        iterate, embed, drift_coef, noise_coef, noise_here = inputs
        drift = drift_of(iterate, embed)
        running = running + drift_coef * drift + noise_coef * noise_here.astype(jnp.float32)
        return running, iterates[0] + running

    start_sum = jnp.zeros((SHOWERS, CELLS, D), jnp.float32)
    final_sum, outputs = lax.scan(advance, start_sum, (iterates, step_embed, drift_scale, noise_scale, noise_draws))
    return outputs
```

```python
import jax
import jax.numpy as jnp
from jax import lax
from jax.experimental import pallas as pl
from jax.experimental.pallas import tpu as pltpu
from jax.sharding import PartitionSpec as P

F32 = jnp.float32
BF16 = jnp.bfloat16
COLS = 8
ROWS = 4

VMEM = pl.BlockSpec(memory_space=pltpu.VMEM)
SMEM = pl.BlockSpec(memory_space=pltpu.SMEM)


def dot(a, b):
    return jnp.dot(a, b, preferred_element_type=F32)


def vmem_call(body, outs, in_specs, name):
    return pl.pallas_call(
        body,
        out_shape=outs,
        in_specs=in_specs,
        out_specs=jax.tree.map(lambda _: VMEM, outs),
        name=name,
    )


def pack(iterates, send_blocks, block):
    steps, showers, cells, width = iterates.shape
    rounds, sent = send_blocks.shape[1:]
    rows = steps * showers

    def body(blocks_ref, it_ref, h_ref, *send_refs):
        for row in range(rows):
            h_ref[row] = it_ref[row // showers, row % showers].astype(BF16)
        for r in range(rounds):
            for k in range(sent):
                at = pl.ds(blocks_ref[0, r, k] * block, block)
                for row in range(rows):
                    send_refs[r][row, k] = h_ref[row, at, :]

    send = jax.ShapeDtypeStruct((rows, sent, block, width), BF16)
    outs = [jax.ShapeDtypeStruct((rows, cells, width), BF16)] + [send] * rounds
    return vmem_call(body, outs, [SMEM, VMEM], "pack")(send_blocks, iterates)


def near(hidden, incoming, embed, weight, columns, tiles, remote, receive):
    rows, cells, width = hidden.shape
    parts, per_row, block, _ = tiles.shape
    sent = incoming.shape[1]
    repeat = rows // embed.shape[0]

    def body(col_ref, recv_ref, h_ref, in_ref, emb_ref, w_ref, tile_ref, rem_ref, agg_ref, pre_ref):
        for b in range(parts):
            wide = jnp.concatenate([tile_ref[b, j] for j in range(per_row)], axis=1)
            for row in range(rows):
                tall = jnp.concatenate(
                    [h_ref[row, pl.ds(col_ref[b, j] * block, block), :] for j in range(per_row)], axis=0
                )
                agg_ref[row, b * block : (b + 1) * block, :] = dot(wide, tall)
        for k in range(sent):
            at = pl.ds(recv_ref[0, 0, k] * block, block)
            for row in range(rows):
                agg_ref[row, at, :] += dot(rem_ref[0, 0, k], in_ref[row, k])
        for row in range(rows):
            pre_ref[row] = dot(h_ref[row], w_ref[...]) + emb_ref[row // repeat][None, :]

    out = jax.ShapeDtypeStruct((rows, cells, width), F32)
    return vmem_call(body, [out, out], [SMEM, SMEM] + [VMEM] * 6, "near")(
        columns, receive, hidden, incoming, embed, weight, tiles, remote
    )


def update(recv_ref, h_ref, in_ref, agg_ref, pre_ref, wn_ref, wo_ref, rem_ref, sum_ref, row):
    sent, block = in_ref.shape[1], in_ref.shape[2]
    sum_ref[...] = agg_ref[row]
    for k in range(sent):
        at = pl.ds(recv_ref[0, 1, k] * block, block)
        sum_ref[at, :] += dot(rem_ref[0, 1, k], in_ref[row, k])
    preact = pre_ref[row] + dot(sum_ref[...].astype(BF16), wn_ref[...])
    half = 0.5 * preact
    activated = (half + half * jnp.tanh(half)).astype(BF16)
    return (h_ref[row].astype(F32) + dot(activated, wo_ref[...])).astype(BF16)


def far(hidden, incoming, agg, pre, neighbor, output, remote, receive, send_blocks):
    rows, cells, width = hidden.shape
    rounds, sent = send_blocks.shape[1:]
    block = incoming.shape[2]

    def body(recv_ref, blocks_ref, h_ref, in_ref, agg_ref, pre_ref, wn_ref, wo_ref, rem_ref, out_ref, s0, s1, sum_ref):
        send_refs = (s0, s1)
        for row in range(rows):
            out_ref[row] = update(recv_ref, h_ref, in_ref, agg_ref, pre_ref, wn_ref, wo_ref, rem_ref, sum_ref, row)
            for r in range(rounds):
                for k in range(sent):
                    send_refs[r][row, k] = out_ref[row, pl.ds(blocks_ref[0, r, k] * block, block), :]

    send = jax.ShapeDtypeStruct((rows, sent, block, width), BF16)
    outs = [jax.ShapeDtypeStruct((rows, cells, width), BF16)] + [send] * rounds
    return pl.pallas_call(
        body,
        out_shape=outs,
        in_specs=[SMEM, SMEM] + [VMEM] * 7,
        out_specs=[VMEM] * len(outs),
        scratch_shapes=[pltpu.VMEM((cells, width), F32)],
        name="far",
    )(receive, send_blocks, hidden, incoming, agg, pre, neighbor, output, remote)


def finish(hidden, incoming, agg, pre, neighbor, output, remote, receive, drift_weight, scale, noise_part):
    rows, cells, width = hidden.shape
    steps = scale.shape[0]
    showers = rows // steps

    def body(recv_ref, scale_ref, h_ref, in_ref, agg_ref, pre_ref, wn_ref, wo_ref, rem_ref, wd_ref, nz_ref, run_ref, tot_ref, sum_ref):
        for shower in range(showers):
            total = None
            for step in range(steps):
                row = step * showers + shower
                last = update(recv_ref, h_ref, in_ref, agg_ref, pre_ref, wn_ref, wo_ref, rem_ref, sum_ref, row)
                drift = scale_ref[step] * dot(last, wd_ref[...])
                total = drift if total is None else total + drift
                run_ref[row] = total + nz_ref[row]
            tot_ref[shower] = run_ref[(steps - 1) * showers + shower].astype(BF16)

    outs = [
        jax.ShapeDtypeStruct((rows, cells, width), F32),
        jax.ShapeDtypeStruct((showers, cells, width), BF16),
    ]
    return pl.pallas_call(
        body,
        out_shape=outs,
        in_specs=[SMEM, SMEM] + [VMEM] * 9,
        out_specs=[VMEM] * 2,
        scratch_shapes=[pltpu.VMEM((cells, width), F32)],
        name="finish",
    )(receive, scale, hidden, incoming, agg, pre, neighbor, output, remote, drift_weight, noise_part)


def row_total(parts):
    def body(p_ref, o_ref):
        total = p_ref[0].astype(F32)
        for z in range(1, parts.shape[0]):
            total = total + p_ref[z].astype(F32)
        o_ref[...] = total.astype(BF16)

    return vmem_call(body, jax.ShapeDtypeStruct(parts.shape[1:], BF16), [VMEM], "row_total")(parts)


def row_prefix(parts, below):
    def body(p_ref, b0, b1, b2, o_ref):
        total = b0[...].astype(F32) + b1[...].astype(F32) + b2[...].astype(F32)
        for z in range(parts.shape[0]):
            o_ref[z] = total.astype(BF16)
            total = total + p_ref[z].astype(F32)

    return vmem_call(body, jax.ShapeDtypeStruct(parts.shape, BF16), [VMEM] * 4, "row_prefix")(parts, *below)


def local(
    iterates,
    noise_draws,
    drift_scale,
    noise_scale,
    step_embed,
    self_weight,
    neighbor_weight,
    output_weight,
    drift_weight,
    local_columns,
    tile_values,
    send_blocks,
    receive_rows,
    remote_values,
):
    steps, showers, cells, width = iterates.shape
    block = tile_values.shape[2]
    rows = steps * showers
    layers = self_weight.shape[0]
    parts = lax.axis_size("dom")
    near_pairs = [(i, i ^ 1) for i in range(parts)]
    far_pairs = [(i, i ^ 2) for i in range(parts)]
    groups = [[y * COLS + z for z in range(COLS)] for y in range(ROWS)]

    first = (lax.axis_index("tm") == 0).astype(F32)
    noise = noise_scale[:, None, None, None] * noise_draws.astype(F32)
    noise_part = jnp.cumsum(noise, axis=0) + first * iterates[:1]
    noise_part = noise_part.reshape(rows, cells, width)

    hidden, send0, send1 = pack(iterates, send_blocks, block)
    for layer in range(layers):
        in0 = lax.ppermute(send0, "dom", near_pairs)
        in1 = lax.ppermute(send1, "dom", far_pairs)
        agg, pre = near(
            hidden, in0, step_embed, self_weight[layer], local_columns, tile_values, remote_values, receive_rows
        )
        if layer + 1 < layers:
            hidden, send0, send1 = far(
                hidden, in1, agg, pre, neighbor_weight[layer], output_weight[layer], remote_values, receive_rows, send_blocks
            )
    running, total = finish(
        hidden, in1, agg, pre, neighbor_weight[layer], output_weight[layer], remote_values, receive_rows,
        drift_weight, drift_scale, noise_part,
    )
    pieces = total.reshape(COLS, -1, width)
    pieces = lax.all_to_all(pieces, "tm", 0, 0, axis_index_groups=groups)
    whole = row_total(pieces)
    below = [
        lax.ppermute(
            whole, "tm", [(y * COLS + z, (y + up) * COLS + z) for y in range(ROWS - up) for z in range(COLS)]
        )
        for up in range(1, ROWS)
    ]
    earlier = lax.all_to_all(row_prefix(pieces, below), "tm", 0, 0, axis_index_groups=groups)
    earlier = earlier.reshape(showers, cells, width).astype(F32)
    return running.reshape(steps, showers, cells, width) + earlier[None]


def solution(mesh):
    return jax.shard_map(
        local,
        mesh=mesh,
        in_specs=(
            P("tm", None, "dom", None),
            P("tm", None, "dom", None),
            P("tm"),
            P("tm"),
            P("tm", None),
            P(),
            P(),
            P(),
            P(),
            P("dom", None),
            P("dom", None, None, None),
            P("dom", None, None),
            P("dom", None, None),
            P("dom", None, None, None, None),
        ),
        out_specs=P("tm", None, "dom", None),
        check_vma=False,
    )
```

```python
import jax
import jax.numpy as jnp
from jax import lax
from jax.experimental import pallas as pl
from jax.experimental.pallas import tpu as pltpu
from jax.sharding import PartitionSpec as P

F32 = jnp.float32
BF16 = jnp.bfloat16
COLS = 8
ROWS = 4


def dot(a, b):
    return jnp.dot(a, b, preferred_element_type=F32)


def call(body, name, outs, scalars, arrays, far_arrays=(), far_outs=(), after=(), scratch=(), flops=1 << 20):
    pin = lambda a: pltpu.with_memory_space_constraint(a, pltpu.VMEM)
    keep = lambda a: pltpu.with_memory_space_constraint(a, pltpu.HBM)
    count = len(scalars) + len(arrays) + len(far_arrays)
    vmem = pl.BlockSpec(memory_space=pltpu.VMEM)

    def inner(*refs):
        body(*refs[:count], *refs[count + len(after) :])

    return pl.pallas_call(
        inner,
        out_shape=[pltpu.VMEM(*o) for o in outs] + [pltpu.HBM(*o) for o in far_outs],
        in_specs=[pl.BlockSpec(memory_space=pltpu.SMEM)] * len(scalars)
        + [vmem] * len(arrays)
        + [pl.BlockSpec(memory_space=pltpu.HBM)] * len(far_arrays)
        + [vmem] * len(after),
        out_specs=[vmem] * len(outs) + [pl.BlockSpec(memory_space=pltpu.HBM)] * len(far_outs),
        scratch_shapes=list(scratch),
        compiler_params=pltpu.CompilerParams(vmem_limit_bytes=12 << 20),
        cost_estimate=pl.CostEstimate(flops=flops, transcendentals=0, bytes_accessed=1 << 10),
        name=name,
    )(*scalars, *map(pin, arrays), *map(keep, far_arrays), *map(pin, after))


def pack(iterates, send_blocks, block):
    steps, showers, cells, width = iterates.shape
    rounds, sent = send_blocks.shape[1:]

    def body(blocks_ref, it_ref, *send_refs):
        for r in reversed(range(rounds)):
            for k in range(sent):
                at = pl.ds(blocks_ref[0, r, k] * block, block)
                for shower in range(showers):
                    for step in range(steps):
                        send_refs[r * showers + shower][step, k] = it_ref[step, shower, at, :].astype(BF16)

    outs = [((steps, sent, block, width), BF16)] * (rounds * showers)
    sends = call(body, "pack", outs, [send_blocks], [iterates])
    return [sends[r * showers : (r + 1) * showers] for r in range(rounds)]


def near_step(col_ref, h_ref, emb_ref, ws, wn, tile_ref, pre_ref, step):
    parts, per_row, block, _ = tile_ref.shape
    mixed = []
    for b in range(parts):
        wide = jnp.concatenate([tile_ref[b, j] for j in range(per_row)], axis=1)
        tall = jnp.concatenate(
            [h_ref[step, pl.ds(col_ref[b, j] * block, block), :] for j in range(per_row)], axis=0
        )
        mixed.append(dot(wide, tall).astype(BF16))
    pre = dot(h_ref[step], ws) + dot(jnp.concatenate(mixed, axis=0), wn)
    pre_ref[step] = pre + emb_ref[step : step + 1, :]


def near(hidden, layer, embed, weight, neighbor, columns, tiles, after):
    steps, cells, width = hidden.shape

    def body(col_ref, h_ref, emb_ref, ws_ref, wn_ref, tile_ref, pre_ref):
        for step in range(steps):
            near_step(col_ref, h_ref, emb_ref, ws_ref[layer], wn_ref[layer], tile_ref, pre_ref, step)

    return call(
        body, "near", [((steps, cells, width), F32)], [columns], [hidden, embed, weight, neighbor, tiles], after=after
    )[0]


def near_first(iterates, shower, embed, weight, neighbor, columns, tiles, after):
    steps, _, cells, width = iterates.shape

    def body(col_ref, it_ref, emb_ref, ws_ref, wn_ref, tile_ref, pre_ref, h_ref):
        for step in range(steps):
            h_ref[step] = it_ref[step, shower].astype(BF16)
        for step in range(steps):
            near_step(col_ref, h_ref, emb_ref, ws_ref[0], wn_ref[0], tile_ref, pre_ref, step)

    return call(
        body, "near_first", [((steps, cells, width), F32), ((steps, cells, width), BF16)], [columns],
        [iterates, embed, weight, neighbor, tiles], after=after,
    )


def update(recv_ref, h_ref, in_refs, pre_ref, wn, wo, rem_ref, step):
    sent, block = in_refs[0].shape[1:3]
    parts = h_ref.shape[1] // block
    addends = [
        (recv_ref[0, r, k], dot(rem_ref[0, r, k], in_ref[step, k])) for r, in_ref in enumerate(in_refs) for k in range(sent)
    ]
    mixed = []
    for b in range(parts):
        total = None
        for row, addend in addends:
            term = jnp.where(row == b, 1.0, 0.0) * addend
            total = term if total is None else total + term
        mixed.append(total.astype(BF16))
    half = 0.5 * (pre_ref[step] + dot(jnp.concatenate(mixed, axis=0), wn))
    activated = (half + half * jnp.tanh(half)).astype(BF16)
    return (h_ref[step].astype(F32) + dot(activated, wo)).astype(BF16)


def far(hidden, incoming, pre, layer, neighbor, output, remote, receive, send_blocks, after):
    steps, cells, width = hidden.shape
    rounds, sent = send_blocks.shape[1:]
    block = incoming[0].shape[2]

    def body(recv_ref, blocks_ref, h_ref, *refs):
        in_refs, (pre_ref, wn_ref, wo_ref, rem_ref, out_ref, *send_refs) = refs[:rounds], refs[rounds:]
        for step in range(steps):
            out_ref[step] = update(recv_ref, h_ref, in_refs, pre_ref, wn_ref[layer], wo_ref[layer], rem_ref, step)
        for r in range(rounds):
            for k in range(sent):
                at = pl.ds(blocks_ref[0, r, k] * block, block)
                for step in range(steps):
                    send_refs[r][step, k] = out_ref[step, at, :]

    outs = [((steps, cells, width), BF16)] + [((steps, sent, block, width), BF16)] * rounds
    return call(
        body, "far", outs, [receive, send_blocks], [hidden, *incoming, pre, neighbor, output, remote], after=after
    )


def finish(hidden, incoming, pre, layer, shower, neighbor, output, remote, receive, drift_weight, scales, noise, iterates, after):
    steps, cells, width = hidden.shape

    def body(recv_ref, ds_ref, ns_ref, h_ref, *refs):
        in_refs, refs = refs[: len(incoming)], refs[len(incoming) :]
        pre_ref, wn_ref, wo_ref, rem_ref, wd_ref, nz_hbm, it_hbm, tot_ref, run_hbm, nz_ref, it_ref, run_ref, sems = refs
        loads = [pltpu.make_async_copy(it_hbm.at[0, shower], it_ref, sems.at[0])]
        loads += [pltpu.make_async_copy(nz_hbm.at[step, shower], nz_ref.at[step], sems.at[1 + step]) for step in range(steps)]
        stores = [pltpu.make_async_copy(run_ref.at[step], run_hbm.at[step], sems.at[1 + steps + step]) for step in range(steps)]
        for load in loads:
            load.start()
        first = jnp.where(lax.axis_index("tm") == 0, 1.0, 0.0)
        total = None
        for step in range(steps):
            last = update(recv_ref, h_ref, in_refs, pre_ref, wn_ref[layer], wo_ref[layer], rem_ref, step)
            drift = ds_ref[step] * dot(last, wd_ref[...])
            if step == 0:
                loads[0].wait()
            loads[1 + step].wait()
            before = first * it_ref[...] if step == 0 else run_ref[step - 1]
            total = before + drift + ns_ref[step] * nz_ref[step].astype(F32)
            run_ref[step] = total
            stores[step].start()
        tot_ref[...] = total.astype(BF16)
        for store in stores:
            store.wait()

    return call(
        body, "finish", [((cells, width), BF16)], [receive, *scales],
        [hidden, *incoming, pre, neighbor, output, remote, drift_weight], [noise, iterates],
        [((steps, cells, width), F32)], after=after, flops=1 << 35,
        scratch=[
            pltpu.VMEM((steps, cells, width), BF16), pltpu.VMEM((cells, width), F32),
            pltpu.VMEM((steps, cells, width), F32), pltpu.SemaphoreType.DMA((1 + 2 * steps,)),
        ],
    )


def row_total(parts):
    def body(p_ref, o_ref):
        total = p_ref[0].astype(F32)
        for z in range(1, parts.shape[0]):
            total = total + p_ref[z].astype(F32)
        o_ref[...] = total.astype(BF16)

    return call(body, "row_total", [(parts.shape[1:], BF16)], [], [parts])[0]


def row_prefix(parts, below):
    def body(p_ref, *refs):
        o_ref = refs[-1]
        total = refs[0][...].astype(F32)
        for ref in refs[1:-1]:
            total = total + ref[...].astype(F32)
        for z in range(parts.shape[0]):
            o_ref[z] = total.astype(BF16)
            total = total + p_ref[z].astype(F32)

    return call(body, "row_prefix", [(parts.shape, BF16)], [], [parts, *below])[0]


def deliver(out, running, earlier, shower, shape):
    steps, cells, width = running.shape
    args = [running, earlier] + ([] if out is None else [out])

    def body(run_ref, early_ref, *refs):
        refs[-1][0, 0] = run_ref[0] + early_ref[...].astype(F32)

    return pl.pallas_call(
        body,
        grid=(steps,),
        out_shape=jax.ShapeDtypeStruct(shape, F32),
        in_specs=[pl.BlockSpec((1, cells, width), lambda t: (t, 0, 0)), pl.BlockSpec((cells, width), lambda t: (0, 0))]
        + [pl.BlockSpec(memory_space=pl.ANY)] * (len(args) - 2),
        out_specs=pl.BlockSpec((1, 1, cells, width), lambda t: (t, shower, 0, 0)),
        input_output_aliases={} if out is None else {2: 0},
        compiler_params=pltpu.CompilerParams(vmem_limit_bytes=12 << 20),
        name="deliver",
    )(*args)


def local(
    iterates,
    noise_draws,
    drift_scale,
    noise_scale,
    step_embed,
    self_weight,
    neighbor_weight,
    output_weight,
    drift_weight,
    local_columns,
    tile_values,
    send_blocks,
    receive_rows,
    remote_values,
):
    steps, showers, cells, width = iterates.shape
    block = tile_values.shape[2]
    layers = self_weight.shape[0]
    parts = lax.axis_size("dom")
    pairs = [[(i, i ^ (1 << r)) for i in range(parts)] for r in range(2)]
    groups = [[y * COLS + z for z in range(COLS)] for y in range(ROWS)]

    sends = pack(iterates, send_blocks, block)
    incoming = [[lax.ppermute(sends[r][s], "dom", pairs[r]) for r in (0, 1)] for s in range(showers)]
    common = (step_embed, self_weight, neighbor_weight, local_columns, tile_values)
    rest = (neighbor_weight, output_weight, remote_values, receive_rows)
    hidden, pre = [None] * showers, [None] * showers
    token = ()
    for s in range(showers):
        pre[s], hidden[s] = near_first(iterates, s, *common, token)
        token = (pre[s],)
    for layer in range(1, layers):
        for s in range(showers):
            hidden[s], *sends = far(hidden[s], incoming[s], pre[s], layer - 1, *rest, send_blocks, token)
            incoming[s] = [lax.ppermute(sends[r], "dom", pairs[r]) for r in (0, 1)]
            pre[s] = near(hidden[s], layer, *common, ())
            token = (pre[s],)
    running, pieces, totals = [None] * showers, [None] * showers, [None] * showers
    for s in range(showers):
        totals[s], running[s] = finish(
            hidden[s], incoming[s], pre[s], layers - 1, s, *rest, drift_weight, (drift_scale, noise_scale),
            noise_draws, iterates, token,
        )
        token = (totals[s],)
        pieces[s] = lax.all_to_all(totals[s].reshape(COLS, -1, width), "tm", 0, 0, axis_index_groups=groups)
    out = None
    for s in range(showers):
        whole = row_total(pieces[s])
        below = [
            lax.ppermute(
                whole, "tm", [(y * COLS + z, (y + up) * COLS + z) for y in range(ROWS - up) for z in range(COLS)]
            )
            for up in range(1, ROWS)
        ]
        earlier = lax.all_to_all(row_prefix(pieces[s], below), "tm", 0, 0, axis_index_groups=groups)
        out = deliver(out, running[s], earlier.reshape(cells, width), s, iterates.shape)
    return out


def solution(mesh):
    return jax.shard_map(
        local,
        mesh=mesh,
        in_specs=(
            P("tm", None, "dom", None),
            P("tm", None, "dom", None),
            P("tm"),
            P("tm"),
            P("tm", None),
            P(),
            P(),
            P(),
            P(),
            P("dom", None),
            P("dom", None, None, None),
            P("dom", None, None),
            P("dom", None, None),
            P("dom", None, None, None, None),
        ),
        out_specs=P("tm", None, "dom", None),
        check_vma=False,
    )
```

```python
import jax
import jax.numpy as jnp
from jax import lax
from jax.experimental import pallas as pl
from jax.experimental.pallas import tpu as pltpu
from jax.sharding import PartitionSpec as P

F32 = jnp.float32
BF16 = jnp.bfloat16


def dot(a, b):
    return jnp.dot(a, b, preferred_element_type=F32)


def call(body, name, outs, scalars, arrays, far_arrays=(), far_outs=(), after=(), scratch=(), aliases=None):
    pin = lambda a: pltpu.with_memory_space_constraint(a, pltpu.VMEM)
    keep = lambda a: pltpu.with_memory_space_constraint(a, pltpu.HBM)
    count = len(scalars) + len(arrays) + len(far_arrays)
    vmem = pl.BlockSpec(memory_space=pltpu.VMEM)

    def inner(*refs):
        body(*refs[:count], *refs[count + len(after) :])

    return pl.pallas_call(
        inner,
        out_shape=[pltpu.VMEM(*o) for o in outs] + [pltpu.HBM(*o) for o in far_outs],
        in_specs=[pl.BlockSpec(memory_space=pltpu.SMEM)] * len(scalars)
        + [vmem] * len(arrays)
        + [pl.BlockSpec(memory_space=pltpu.HBM)] * len(far_arrays)
        + [vmem] * len(after),
        out_specs=[vmem] * len(outs) + [pl.BlockSpec(memory_space=pltpu.HBM)] * len(far_outs),
        scratch_shapes=list(scratch),
        input_output_aliases=aliases or {},
        compiler_params=pltpu.CompilerParams(vmem_limit_bytes=12 << 20),
        cost_estimate=pl.CostEstimate(flops=1 << 20, transcendentals=0, bytes_accessed=1 << 10),
        name=name,
    )(*scalars, *map(pin, arrays), *map(keep, far_arrays), *map(pin, after))


def pack(iterates, shower, send_blocks, block):
    steps, _, cells, width = iterates.shape
    rounds, sent = send_blocks.shape[1:]

    def body(blocks_hbm, it_hbm, *refs):
        send_refs, (blocks_ref, it_ref, sems) = refs[:rounds], refs[rounds:]
        index = pltpu.make_async_copy(blocks_hbm, blocks_ref, sems.at[steps])
        index.start()
        loads = [pltpu.make_async_copy(it_hbm.at[step, shower], it_ref.at[step], sems.at[step]) for step in range(steps)]
        for load in loads:
            load.start()
        index.wait()
        for step in range(steps):
            loads[step].wait()
            for r in range(rounds):
                for k in range(sent):
                    at = pl.ds(blocks_ref[0, r, k] * block, block)
                    send_refs[r][step, k] = it_ref[step, at, :].astype(BF16)

    return call(
        body, "pack", [((steps, sent, block, width), BF16)] * rounds, [], [], [send_blocks, iterates],
        scratch=[
            pltpu.SMEM(send_blocks.shape, jnp.int32), pltpu.VMEM((steps, cells, width), F32),
            pltpu.SemaphoreType.DMA((steps + 1,)),
        ],
    )


def near_step(col_ref, h_ref, emb_ref, ws, wn, tile_ref, pre_ref, step):
    parts, per_row, block, _ = tile_ref.shape
    mixed = []
    for b in range(parts):
        wide = jnp.concatenate([tile_ref[b, j] for j in range(per_row)], axis=1)
        tall = jnp.concatenate(
            [h_ref[step, pl.ds(col_ref[b, j] * block, block), :] for j in range(per_row)], axis=0
        )
        mixed.append(dot(wide, tall).astype(BF16))
    pre = dot(h_ref[step], ws) + dot(jnp.concatenate(mixed, axis=0), wn)
    pre_ref[step] = pre + emb_ref[step : step + 1, :]


def near(hidden, layer, embed, weight, neighbor, columns, tiles, after):
    steps, cells, width = hidden.shape

    def body(col_ref, h_ref, emb_ref, ws_ref, wn_ref, tile_ref, pre_ref):
        for step in range(steps):
            near_step(col_ref, h_ref, emb_ref, ws_ref[layer], wn_ref[layer], tile_ref, pre_ref, step)

    return call(
        body, "near", [((steps, cells, width), F32)], [columns], [hidden, embed, weight, neighbor, tiles], after=after
    )[0]


def near_first(iterates, shower, embed, weight, neighbor, columns, tiles, after):
    steps, _, cells, width = iterates.shape

    def body(col_ref, it_ref, emb_ref, ws_ref, wn_ref, tile_ref, pre_ref, h_ref):
        for step in range(steps):
            h_ref[step] = it_ref[step, shower].astype(BF16)
        for step in range(steps):
            near_step(col_ref, h_ref, emb_ref, ws_ref[0], wn_ref[0], tile_ref, pre_ref, step)

    return call(
        body, "near_first", [((steps, cells, width), F32), ((steps, cells, width), BF16)], [columns],
        [iterates, embed, weight, neighbor, tiles], after=after,
    )


def update(recv_ref, h_ref, in_refs, pre_ref, wn, wo, rem_ref, step):
    sent, block = in_refs[0].shape[1:3]
    parts = h_ref.shape[1] // block
    addends = [
        (recv_ref[0, r, k], dot(rem_ref[0, r, k], in_ref[step, k])) for r, in_ref in enumerate(in_refs) for k in range(sent)
    ]
    mixed = []
    for b in range(parts):
        total = None
        for row, addend in addends:
            term = jnp.where(row == b, 1.0, 0.0) * addend
            total = term if total is None else total + term
        mixed.append(total.astype(BF16))
    half = 0.5 * (pre_ref[step] + dot(jnp.concatenate(mixed, axis=0), wn))
    activated = (half + half * jnp.tanh(half)).astype(BF16)
    return (h_ref[step].astype(F32) + dot(activated, wo)).astype(BF16)


def far(hidden, incoming, pre, layer, neighbor, output, remote, receive, send_blocks, after):
    steps, cells, width = hidden.shape
    rounds, sent = send_blocks.shape[1:]
    block = incoming[0].shape[2]

    def body(recv_ref, blocks_ref, h_ref, *refs):
        in_refs, (pre_ref, wn_ref, wo_ref, rem_ref, out_ref, *send_refs) = refs[:rounds], refs[rounds:]
        for step in range(steps):
            out_ref[step] = update(recv_ref, h_ref, in_refs, pre_ref, wn_ref[layer], wo_ref[layer], rem_ref, step)
        for r in range(rounds):
            for k in range(sent):
                at = pl.ds(blocks_ref[0, r, k] * block, block)
                for step in range(steps):
                    send_refs[r][step, k] = out_ref[step, at, :]

    outs = [((steps, cells, width), BF16)] + [((steps, sent, block, width), BF16)] * rounds
    return call(
        body, "far", outs, [receive, send_blocks], [hidden, *incoming, pre, neighbor, output, remote], after=after
    )


def noise_sums(noise, scale, iterates, after):
    steps, showers, cells, width = noise.shape

    def body(scale_ref, nz_hbm, it_hbm, *refs):
        out_refs, (nz_ref, it_ref, sems) = refs[:showers], refs[showers:]
        loads = [pltpu.make_async_copy(it_hbm.at[0], it_ref, sems.at[0]), pltpu.make_async_copy(nz_hbm, nz_ref, sems.at[1])]
        for load in loads:
            load.start()
        for load in loads:
            load.wait()
        first = jnp.where(lax.axis_index("tm") == 0, 1.0, 0.0)
        for shower in range(showers):
            total = first * it_ref[shower]
            for step in range(steps):
                total = total + scale_ref[step] * nz_ref[step, shower].astype(F32)
                out_refs[shower][step] = total

    return call(
        body, "noise_sums", [((steps, cells, width), F32)] * showers, [scale], [], [noise, iterates], after=after,
        scratch=[
            pltpu.VMEM(noise.shape, BF16), pltpu.VMEM(iterates.shape[1:], F32), pltpu.SemaphoreType.DMA((2,)),
        ],
    )


def finish(hidden, incoming, pre, layer, shower, showers, neighbor, output, remote, receive, drift_weight, scale, noise_sum, totals, after):
    steps, cells, width = hidden.shape
    rounds = len(incoming)

    def body(recv_ref, scale_ref, h_ref, *refs):
        in_refs, (pre_ref, wn_ref, wo_ref, rem_ref, wd_ref, nz_ref, *_, tot_ref, run_ref) = refs[:rounds], refs[rounds:]
        drift = None
        for step in range(steps):
            last = update(recv_ref, h_ref, in_refs, pre_ref, wn_ref[layer], wo_ref[layer], rem_ref, step)
            term = scale_ref[step] * dot(last, wd_ref[...])
            drift = term if drift is None else drift + term
            run = drift + nz_ref[step]
            run_ref[step] = run
        tot_ref[shower] = run.astype(BF16)

    arrays = [hidden, *incoming, pre, neighbor, output, remote, drift_weight, noise_sum, *totals]
    return call(
        body, "finish", [((showers, cells, width), BF16), ((steps, cells, width), F32)], [receive, scale], arrays,
        after=after, aliases={len(arrays) + 1: 0} if totals else None,
    )


def exclusive_prefix(parts):
    def body(p_ref, o_ref):
        total = jnp.zeros(parts.shape[1:], F32)
        for k in range(parts.shape[0]):
            o_ref[k] = total.astype(BF16)
            total = total + p_ref[k].astype(F32)

    return call(body, "exclusive_prefix", [(parts.shape, BF16)], [], [parts])[0]


def deliver(running, earlier):
    showers = len(running)
    steps, cells, width = running[0].shape
    every = [(step, shower) for step in range(steps) for shower in range(showers)]

    def body(*refs):
        run_refs, (early_ref, out_hbm, out_ref, sems) = refs[:showers], refs[showers:]
        stores = [
            pltpu.make_async_copy(out_ref.at[step, shower], out_hbm.at[step, shower], sems.at[i])
            for i, (step, shower) in enumerate(every)
        ]
        for i, (step, shower) in enumerate(every):
            out_ref[step, shower] = run_refs[shower][step] + early_ref[shower].astype(F32)
            stores[i].start()
        for store in stores:
            store.wait()

    shape = (steps, showers, cells, width)
    return call(
        body, "deliver", [], [], [*running, earlier], [], [(shape, F32)],
        scratch=[pltpu.VMEM(shape, F32), pltpu.SemaphoreType.DMA((len(every),))],
    )[0]


def local(
    iterates,
    noise_draws,
    drift_scale,
    noise_scale,
    step_embed,
    self_weight,
    neighbor_weight,
    output_weight,
    drift_weight,
    local_columns,
    tile_values,
    send_blocks,
    receive_rows,
    remote_values,
):
    steps, showers, cells, width = iterates.shape
    block = tile_values.shape[2]
    layers = self_weight.shape[0]
    parts = lax.axis_size("dom")
    pairs = [[(i, i ^ (1 << r)) for i in range(parts)] for r in range(2)]
    incoming = []
    for s in range(showers):
        sends = pack(iterates, s, send_blocks, block)
        incoming.append([lax.ppermute(sends[r], "dom", pairs[r]) for r in (0, 1)])
    common = (step_embed, self_weight, neighbor_weight, local_columns, tile_values)
    rest = (neighbor_weight, output_weight, remote_values, receive_rows)
    hidden, pre = [None] * showers, [None] * showers
    token = ()
    for s in range(showers):
        pre[s], hidden[s] = near_first(iterates, s, *common, token)
        token = (pre[s],)
    noise_sum = noise_sums(noise_draws, noise_scale, iterates, token)
    token = (noise_sum[0],)
    for layer in range(1, layers):
        for s in range(showers):
            hidden[s], *sends = far(hidden[s], incoming[s], pre[s], layer - 1, *rest, send_blocks, token)
            incoming[s] = [lax.ppermute(sends[r], "dom", pairs[r]) for r in (0, 1)]
            pre[s] = near(hidden[s], layer, *common, ())
            token = (pre[s],)
    totals, running = (), [None] * showers
    for s in range(showers):
        total, running[s] = finish(
            hidden[s], incoming[s], pre[s], layers - 1, s, showers, *rest, drift_weight, drift_scale, noise_sum[s],
            totals, token,
        )
        totals, token = (total,), ()
    pieces = lax.all_to_all(total.reshape(lax.axis_size("tm"), -1, width), "tm", 0, 0)
    earlier = lax.all_to_all(exclusive_prefix(pieces), "tm", 0, 0)
    return deliver(running, earlier.reshape(showers, cells, width))


def solution(mesh):
    return jax.shard_map(
        local,
        mesh=mesh,
        in_specs=(
            P("tm", None, "dom", None),
            P("tm", None, "dom", None),
            P("tm"),
            P("tm"),
            P("tm", None),
            P(),
            P(),
            P(),
            P(),
            P("dom", None),
            P("dom", None, None, None),
            P("dom", None, None),
            P("dom", None, None),
            P("dom", None, None, None, None),
        ),
        out_specs=P("tm", None, "dom", None),
        check_vma=False,
    )
```

```python
import jax
import jax.numpy as jnp
from jax import lax
from jax.experimental import pallas as pl
from jax.experimental.pallas import tpu as pltpu
from jax.sharding import PartitionSpec as P

F32 = jnp.float32
BF16 = jnp.bfloat16


def dot(a, b):
    return jnp.dot(a, b, preferred_element_type=F32)


def call(body, name, outs, scalars, arrays, far_arrays=(), far_outs=(), after=(), scratch=(), aliases=None):
    pin = lambda a: pltpu.with_memory_space_constraint(a, pltpu.VMEM)
    keep = lambda a: pltpu.with_memory_space_constraint(a, pltpu.HBM)
    count = len(scalars) + len(arrays) + len(far_arrays)
    vmem = pl.BlockSpec(memory_space=pltpu.VMEM)

    def inner(*refs):
        body(*refs[:count], *refs[count + len(after) :])

    return pl.pallas_call(
        inner,
        out_shape=[pltpu.VMEM(*o) for o in outs] + [pltpu.HBM(*o) for o in far_outs],
        in_specs=[pl.BlockSpec(memory_space=pltpu.SMEM)] * len(scalars)
        + [vmem] * len(arrays)
        + [pl.BlockSpec(memory_space=pltpu.HBM)] * len(far_arrays)
        + [vmem] * len(after),
        out_specs=[vmem] * len(outs) + [pl.BlockSpec(memory_space=pltpu.HBM)] * len(far_outs),
        scratch_shapes=list(scratch),
        input_output_aliases=aliases or {},
        compiler_params=pltpu.CompilerParams(vmem_limit_bytes=12 << 20),
        cost_estimate=pl.CostEstimate(flops=1 << 20, transcendentals=0, bytes_accessed=1 << 10),
        name=name,
    )(*scalars, *map(pin, arrays), *map(keep, far_arrays), *map(pin, after))


def pack(iterates, shower, send_blocks, block, after):
    steps, _, cells, width = iterates.shape
    rounds, sent = send_blocks.shape[1:]

    def body(blocks_hbm, it_hbm, *refs):
        send_refs, (blocks_ref, it_ref, sems) = refs[:rounds], refs[rounds:]
        index = pltpu.make_async_copy(blocks_hbm, blocks_ref, sems.at[steps])
        index.start()
        loads = [pltpu.make_async_copy(it_hbm.at[step, shower], it_ref.at[step], sems.at[step]) for step in range(steps)]
        for load in loads:
            load.start()
        index.wait()
        for step in range(steps):
            loads[step].wait()
            for r in range(rounds):
                for k in range(sent):
                    at = pl.ds(blocks_ref[0, r, k] * block, block)
                    send_refs[r][step, k] = it_ref[step, at, :].astype(BF16)

    return call(
        body, "pack", [((steps, sent, block, width), BF16)] * rounds, [], [], [send_blocks, iterates], after=after,
        scratch=[
            pltpu.SMEM(send_blocks.shape, jnp.int32), pltpu.VMEM((steps, cells, width), F32),
            pltpu.SemaphoreType.DMA((steps + 1,)),
        ],
    )


def near_step(col_ref, h_ref, emb_ref, ws, wn, tile_ref, pre_ref, step):
    parts, per_row, block, _ = tile_ref.shape
    mixed = []
    for b in range(parts):
        wide = jnp.concatenate([tile_ref[b, j] for j in range(per_row)], axis=1)
        tall = jnp.concatenate(
            [h_ref[step, pl.ds(col_ref[b, j] * block, block), :] for j in range(per_row)], axis=0
        )
        mixed.append(dot(wide, tall).astype(BF16))
    pre = dot(h_ref[step], ws) + dot(jnp.concatenate(mixed, axis=0), wn)
    pre_ref[step] = pre + emb_ref[step : step + 1, :]


def near(hidden, layer, embed, weight, neighbor, columns, tiles, after):
    steps, cells, width = hidden.shape

    def body(col_ref, h_ref, emb_ref, ws_ref, wn_ref, tile_ref, pre_ref):
        for step in range(steps):
            near_step(col_ref, h_ref, emb_ref, ws_ref[layer], wn_ref[layer], tile_ref, pre_ref, step)

    return call(
        body, "near", [((steps, cells, width), F32)], [columns], [hidden, embed, weight, neighbor, tiles], after=after
    )[0]


def near_first(iterates, shower, embed, weight, neighbor, columns, tiles, after):
    steps, _, cells, width = iterates.shape

    def body(col_ref, it_ref, emb_ref, ws_ref, wn_ref, tile_ref, pre_ref, h_ref):
        for step in range(steps):
            h_ref[step] = it_ref[step, shower].astype(BF16)
        for step in range(steps):
            near_step(col_ref, h_ref, emb_ref, ws_ref[0], wn_ref[0], tile_ref, pre_ref, step)

    return call(
        body, "near_first", [((steps, cells, width), F32), ((steps, cells, width), BF16)], [columns],
        [iterates, embed, weight, neighbor, tiles], after=after,
    )


def update(recv_ref, h_ref, in_refs, pre_ref, wn, wo, rem_ref, step):
    sent, block = in_refs[0].shape[1:3]
    parts = h_ref.shape[1] // block
    even = lax.rem(lax.axis_index("dom"), 2) == 0
    addends = []
    for r in range(2):
        for k in range(sent):
            chosen = in_refs[r][step, k]
            if r == 1 and len(in_refs) > 2:
                chosen = jnp.where(even, chosen, in_refs[2 + step][0, k])
            addends.append((recv_ref[0, r, k], dot(rem_ref[0, r, k], chosen)))
    mixed = []
    for b in range(parts):
        total = None
        for row, addend in addends:
            term = jnp.where(row == b, 1.0, 0.0) * addend
            total = term if total is None else total + term
        mixed.append(total.astype(BF16))
    half = 0.5 * (pre_ref[step] + dot(jnp.concatenate(mixed, axis=0), wn))
    activated = (half + half * jnp.tanh(half)).astype(BF16)
    return (h_ref[step].astype(F32) + dot(activated, wo)).astype(BF16)


def far(hidden, incoming, pre, layer, neighbor, output, remote, receive, send_blocks, by_step, after):
    steps, cells, width = hidden.shape
    rounds, sent = send_blocks.shape[1:]
    block = incoming[0].shape[2]
    count = len(incoming)

    def body(recv_ref, blocks_ref, h_ref, *refs):
        in_refs, (pre_ref, wn_ref, wo_ref, rem_ref, out_ref, *send_refs) = refs[:count], refs[count:]
        for step in range(steps):
            out_ref[step] = update(recv_ref, h_ref, in_refs, pre_ref, wn_ref[layer], wo_ref[layer], rem_ref, step)
        for r in range(rounds):
            for k in range(sent):
                at = pl.ds(blocks_ref[0, r, k] * block, block)
                for step in range(steps):
                    rows = out_ref[step, at, :]
                    send_refs[r][step, k] = rows
                    if by_step and r == 1:
                        send_refs[rounds + step][0, k] = rows

    outs = [((steps, cells, width), BF16)] + [((steps, sent, block, width), BF16)] * rounds
    if by_step:
        outs += [((1, sent, block, width), BF16)] * steps
    return call(
        body, "far", outs, [receive, send_blocks], [hidden, *incoming, pre, neighbor, output, remote], after=after
    )


def ready(after):
    def body(o_ref):
        o_ref[...] = jnp.zeros_like(o_ref)

    return call(body, "ready", [((16, 128), BF16)], [], [], after=after)[0]


def hold(arrays, after):
    outs = [(a.shape, a.dtype) for a in arrays]
    return call(lambda *refs: None, "hold", outs, [], arrays, after=after, aliases={i: i for i in range(len(arrays))})


def noise_sums(noise, scale, iterates, after):
    steps, showers, cells, width = noise.shape

    def body(scale_ref, nz_hbm, it_hbm, *refs):
        out_refs, (nz_ref, it_ref, sems) = refs[:showers], refs[showers:]
        loads = [pltpu.make_async_copy(it_hbm.at[0], it_ref, sems.at[0]), pltpu.make_async_copy(nz_hbm, nz_ref, sems.at[1])]
        for load in loads:
            load.start()
        for load in loads:
            load.wait()
        first = jnp.where(lax.axis_index("tm") == 0, 1.0, 0.0)
        for shower in range(showers):
            total = first * it_ref[shower]
            for step in range(steps):
                total = total + scale_ref[step] * nz_ref[step, shower].astype(F32)
                out_refs[shower][step] = total

    return call(
        body, "noise_sums", [((steps, cells, width), F32)] * showers, [scale], [], [noise, iterates], after=after,
        scratch=[
            pltpu.VMEM(noise.shape, BF16), pltpu.VMEM(iterates.shape[1:], F32), pltpu.SemaphoreType.DMA((2,)),
        ],
    )


def finish(hidden, incoming, pre, layer, shower, showers, neighbor, output, remote, receive, drift_weight, scale, noise_sum, totals, after):
    steps, cells, width = hidden.shape
    rounds = len(incoming)

    def body(recv_ref, scale_ref, h_ref, *refs):
        in_refs, (pre_ref, wn_ref, wo_ref, rem_ref, wd_ref, nz_ref, *_, tot_ref, run_ref) = refs[:rounds], refs[rounds:]
        drift = None
        for step in range(steps):
            last = update(recv_ref, h_ref, in_refs, pre_ref, wn_ref[layer], wo_ref[layer], rem_ref, step)
            term = scale_ref[step] * dot(last, wd_ref[...])
            drift = term if drift is None else drift + term
            run = drift + nz_ref[step]
            run_ref[step] = run
        tot_ref[shower] = run.astype(BF16)

    arrays = [hidden, *incoming, pre, neighbor, output, remote, drift_weight, noise_sum, *totals]
    return call(
        body, "finish", [((showers, cells, width), BF16), ((steps, cells, width), F32)], [receive, scale], arrays,
        after=after, aliases={len(arrays) + 1: 0} if totals else None,
    )


def exclusive_prefix(parts):
    def body(p_ref, o_ref):
        total = jnp.zeros(parts.shape[1:], F32)
        for k in range(parts.shape[0]):
            o_ref[k] = total.astype(BF16)
            total = total + p_ref[k].astype(F32)

    return call(body, "exclusive_prefix", [(parts.shape, BF16)], [], [parts])[0]


def deliver(running, earlier):
    showers = len(running)
    steps, cells, width = running[0].shape
    every = [(step, shower) for step in range(steps) for shower in range(showers)]

    def body(*refs):
        run_refs, (early_ref, out_hbm, out_ref, sems) = refs[:showers], refs[showers:]
        stores = [
            pltpu.make_async_copy(out_ref.at[step, shower], out_hbm.at[step, shower], sems.at[i])
            for i, (step, shower) in enumerate(every)
        ]
        for i, (step, shower) in enumerate(every):
            out_ref[step, shower] = run_refs[shower][step] + early_ref[shower].astype(F32)
            stores[i].start()
        for store in stores:
            store.wait()

    shape = (steps, showers, cells, width)
    return call(
        body, "deliver", [], [], [*running, earlier], [], [(shape, F32)],
        scratch=[pltpu.VMEM(shape, F32), pltpu.SemaphoreType.DMA((len(every),))],
    )[0]


def local(
    iterates,
    noise_draws,
    drift_scale,
    noise_scale,
    step_embed,
    self_weight,
    neighbor_weight,
    output_weight,
    drift_weight,
    local_columns,
    tile_values,
    send_blocks,
    receive_rows,
    remote_values,
):
    steps, showers, cells, width = iterates.shape
    block = tile_values.shape[2]
    layers = self_weight.shape[0]
    parts = lax.axis_size("dom")
    pairs = [[(i, i ^ (1 << r)) for i in range(parts)] for r in range(2)]
    incoming, token = [], ()
    for s in range(showers):
        sends = pack(iterates, s, send_blocks, block, token)
        token = (sends[1],)
        incoming.append([lax.ppermute(sends[r], "dom", pairs[r]) for r in (0, 1)])
    common = (step_embed, self_weight, neighbor_weight, local_columns, tile_values)
    rest = (neighbor_weight, output_weight, remote_values, receive_rows)
    hidden, pre = [None] * showers, [None] * showers
    for s in range(showers):
        pre[s], hidden[s] = near_first(iterates, s, *common, token)
        token = (pre[s],)
    evens, odds = ([(i, j) for i, j in pairs[1] if i % 2 == odd] for odd in (0, 1))
    hand_over = [(i, i + 1) for i in range(0, parts, 2)]
    noise_sum = None
    for layer in range(1, layers):
        last = layer + 1 == layers
        held = []
        for s in range(showers):
            hidden[s], send0, send1, *again = far(
                hidden[s], incoming[s], pre[s], layer - 1, *rest, send_blocks, last, token
            )
            held += again
            incoming[s] = [lax.ppermute(send0, "dom", pairs[0]), lax.ppermute(send1, "dom", evens if last else pairs[1])]
            pre[s] = near(hidden[s], layer, *common, ())
            token = (pre[s],)
            if noise_sum is None:
                noise_sum = noise_sums(noise_draws, noise_scale, iterates, token)
                token = (noise_sum[0],)
        if last:
            turn = lax.ppermute(ready((*incoming[0], incoming[-1][0], pre[-1])), "dom", hand_over)
            for i, sends in enumerate(hold(held, (turn,))):
                incoming[i // steps].append(lax.ppermute(sends, "dom", odds))
    totals, running = (), [None] * showers
    for s in range(showers):
        total, running[s] = finish(
            hidden[s], incoming[s], pre[s], layers - 1, s, showers, *rest, drift_weight, drift_scale, noise_sum[s],
            totals, token,
        )
        totals, token = (total,), ()
    pieces = lax.all_to_all(total.reshape(lax.axis_size("tm"), -1, width), "tm", 0, 0)
    earlier = lax.all_to_all(exclusive_prefix(pieces), "tm", 0, 0)
    return deliver(running, earlier.reshape(showers, cells, width))


def solution(mesh):
    return jax.shard_map(
        local,
        mesh=mesh,
        in_specs=(
            P("tm", None, "dom", None),
            P("tm", None, "dom", None),
            P("tm"),
            P("tm"),
            P("tm", None),
            P(),
            P(),
            P(),
            P(),
            P("dom", None),
            P("dom", None, None, None),
            P("dom", None, None),
            P("dom", None, None),
            P("dom", None, None, None, None),
        ),
        out_specs=P("tm", None, "dom", None),
        check_vma=False,
    )
```

```python
import jax
import jax.numpy as jnp
from jax import lax
from jax.experimental import pallas as pl
from jax.experimental.pallas import tpu as pltpu
from jax.sharding import PartitionSpec as P

F32 = jnp.float32
BF16 = jnp.bfloat16


def dot(a, b):
    return jnp.dot(a, b, preferred_element_type=F32)


def call(body, name, outs, scalars, arrays, far_arrays=(), far_outs=(), after=(), scratch=(), aliases=None):
    pin = lambda a: pltpu.with_memory_space_constraint(a, pltpu.VMEM)
    keep = lambda a: pltpu.with_memory_space_constraint(a, pltpu.HBM)
    count = len(scalars) + len(arrays) + len(far_arrays)
    vmem = pl.BlockSpec(memory_space=pltpu.VMEM)

    def inner(*refs):
        body(*refs[:count], *refs[count + len(after) :])

    return pl.pallas_call(
        inner,
        out_shape=[pltpu.VMEM(*o) for o in outs] + [pltpu.HBM(*o) for o in far_outs],
        in_specs=[pl.BlockSpec(memory_space=pltpu.SMEM)] * len(scalars)
        + [vmem] * len(arrays)
        + [pl.BlockSpec(memory_space=pltpu.HBM)] * len(far_arrays)
        + [vmem] * len(after),
        out_specs=[vmem] * len(outs) + [pl.BlockSpec(memory_space=pltpu.HBM)] * len(far_outs),
        scratch_shapes=list(scratch),
        input_output_aliases=aliases or {},
        compiler_params=pltpu.CompilerParams(vmem_limit_bytes=12 << 20),
        cost_estimate=pl.CostEstimate(flops=1 << 20, transcendentals=0, bytes_accessed=1 << 10),
        name=name,
    )(*scalars, *map(pin, arrays), *map(keep, far_arrays), *map(pin, after))


def pack(iterates, shower, send_blocks, block):
    steps, _, cells, width = iterates.shape
    rounds, sent = send_blocks.shape[1:]

    def body(blocks_hbm, it_hbm, *refs):
        send_refs, (blocks_ref, it_ref, sems) = refs[:rounds], refs[rounds:]
        index = pltpu.make_async_copy(blocks_hbm, blocks_ref, sems.at[steps])
        index.start()
        loads = [pltpu.make_async_copy(it_hbm.at[step, shower], it_ref.at[step], sems.at[step]) for step in range(steps)]
        for load in loads:
            load.start()
        index.wait()
        for step in range(steps):
            loads[step].wait()
            for r in range(rounds):
                for k in range(sent):
                    at = pl.ds(blocks_ref[0, r, k] * block, block)
                    send_refs[r][step, k] = it_ref[step, at, :].astype(BF16)

    return call(
        body, "pack", [((steps, sent, block, width), BF16)] * rounds, [], [], [send_blocks, iterates],
        scratch=[
            pltpu.SMEM(send_blocks.shape, jnp.int32), pltpu.VMEM((steps, cells, width), F32),
            pltpu.SemaphoreType.DMA((steps + 1,)),
        ],
    )


def near_step(col_ref, h_ref, emb_ref, ws, wn, tile_ref, pre_ref, step):
    parts, per_row, block, _ = tile_ref.shape
    mixed = []
    for b in range(parts):
        wide = jnp.concatenate([tile_ref[b, j] for j in range(per_row)], axis=1)
        tall = jnp.concatenate(
            [h_ref[step, pl.ds(col_ref[b, j] * block, block), :] for j in range(per_row)], axis=0
        )
        mixed.append(dot(wide, tall).astype(BF16))
    pre = dot(h_ref[step], ws) + dot(jnp.concatenate(mixed, axis=0), wn)
    pre_ref[step] = pre + emb_ref[step : step + 1, :]


def near(hidden, layer, embed, weight, neighbor, columns, tiles, after):
    steps, cells, width = hidden.shape

    def body(col_ref, h_ref, emb_ref, ws_ref, wn_ref, tile_ref, pre_ref):
        for step in range(steps):
            near_step(col_ref, h_ref, emb_ref, ws_ref[layer], wn_ref[layer], tile_ref, pre_ref, step)

    return call(
        body, "near", [((steps, cells, width), F32)], [columns], [hidden, embed, weight, neighbor, tiles], after=after
    )[0]


def near_first(iterates, shower, embed, weight, neighbor, columns, tiles, after):
    steps, _, cells, width = iterates.shape

    def body(col_ref, it_ref, emb_ref, ws_ref, wn_ref, tile_ref, pre_ref, h_ref):
        for step in range(steps):
            h_ref[step] = it_ref[step, shower].astype(BF16)
        for step in range(steps):
            near_step(col_ref, h_ref, emb_ref, ws_ref[0], wn_ref[0], tile_ref, pre_ref, step)

    return call(
        body, "near_first", [((steps, cells, width), F32), ((steps, cells, width), BF16)], [columns],
        [iterates, embed, weight, neighbor, tiles], after=after,
    )


def received(recv_ref, rem_ref, rounds, cells):
    steps, sent, block, _ = next(iter(rounds.values())).shape
    mixed = []
    for step in range(steps):
        addends = [(recv_ref[0, r, k], dot(rem_ref[0, r, k], in_ref[step, k])) for r, in_ref in rounds.items() for k in range(sent)]
        for b in range(cells // block):
            total = None
            for row, addend in addends:
                term = jnp.where(row == b, 1.0, 0.0) * addend
                total = term if total is None else total + term
            mixed.append(total.astype(BF16))
    return jnp.concatenate(mixed, axis=0)


def middle(incoming, pre, layer, neighbor, remote, receive, after):
    shape = pre.shape

    def body(recv_ref, in_ref, pre_ref, wn_ref, rem_ref, out_ref):
        mixed = received(recv_ref, rem_ref, {0: in_ref}, shape[1])
        out_ref[...] = pre_ref[...] + dot(mixed, wn_ref[layer]).reshape(shape)

    return call(body, "middle", [(shape, F32)], [receive], [incoming, pre, neighbor, remote], after=after)[0]


def update(recv_ref, h_ref, rounds, pre_ref, wn, wo, rem_ref):
    steps, cells, width = h_ref.shape
    half = 0.5 * (pre_ref[...].reshape(steps * cells, width) + dot(received(recv_ref, rem_ref, rounds, cells), wn))
    activated = (half + half * jnp.tanh(half)).astype(BF16)
    before = h_ref[...].reshape(steps * cells, width).astype(F32)
    return (before + dot(activated, wo)).astype(BF16)


def far(hidden, incoming, pre, layer, neighbor, output, remote, receive, send_blocks, after):
    steps, cells, width = hidden.shape
    rounds, sent = send_blocks.shape[1:]
    block = incoming[0].shape[2]

    def body(recv_ref, blocks_ref, h_ref, *refs):
        in_refs, (pre_ref, wn_ref, wo_ref, rem_ref, out_ref, *send_refs) = refs[:rounds], refs[rounds:]
        rows = update(recv_ref, h_ref, dict(enumerate(in_refs)), pre_ref, wn_ref[layer], wo_ref[layer], rem_ref)
        out_ref[...] = rows.reshape(steps, cells, width)
        for r in range(rounds):
            for k in range(sent):
                at = pl.ds(blocks_ref[0, r, k] * block, block)
                for step in range(steps):
                    send_refs[r][step, k] = out_ref[step, at, :]

    outs = [((steps, cells, width), BF16)] + [((steps, sent, block, width), BF16)] * rounds
    return call(
        body, "far", outs, [receive, send_blocks], [hidden, *incoming, pre, neighbor, output, remote], after=after
    )


def noise_sums(noise, scale, iterates, after):
    steps, showers, cells, width = noise.shape

    def body(scale_ref, nz_hbm, it_hbm, *refs):
        out_refs, (nz_ref, it_ref, sems) = refs[:showers], refs[showers:]
        loads = [pltpu.make_async_copy(it_hbm.at[0], it_ref, sems.at[0]), pltpu.make_async_copy(nz_hbm, nz_ref, sems.at[1])]
        for load in loads:
            load.start()
        for load in loads:
            load.wait()
        first = jnp.where(lax.axis_index("tm") == 0, 1.0, 0.0)
        for shower in range(showers):
            total = first * it_ref[shower]
            for step in range(steps):
                total = total + scale_ref[step] * nz_ref[step, shower].astype(F32)
                out_refs[shower][step] = total

    return call(
        body, "noise_sums", [((steps, cells, width), F32)] * showers, [scale], [], [noise, iterates], after=after,
        scratch=[
            pltpu.VMEM(noise.shape, BF16), pltpu.VMEM(iterates.shape[1:], F32), pltpu.SemaphoreType.DMA((2,)),
        ],
    )


def finish(hidden, incoming, pre, layer, shower, showers, neighbor, output, remote, receive, drift_weight, scale, noise_sum, totals, after):
    steps, cells, width = hidden.shape

    count = len(incoming)

    def body(recv_ref, scale_ref, h_ref, *refs):
        rounds = dict(zip(incoming, refs[:count]))
        pre_ref, wn_ref, wo_ref, rem_ref, wd_ref, nz_ref, *_, tot_ref, run_ref = refs[count:]
        last = update(recv_ref, h_ref, rounds, pre_ref, wn_ref[layer], wo_ref[layer], rem_ref)
        terms = dot(last, wd_ref[...])
        drift = None
        for step in range(steps):
            term = scale_ref[step] * terms[step * cells : (step + 1) * cells]
            drift = term if drift is None else drift + term
            run = drift + nz_ref[step]
            run_ref[step] = run
        tot_ref[shower] = run.astype(BF16)

    arrays = [hidden, *incoming.values(), pre, neighbor, output, remote, drift_weight, noise_sum, *totals]
    return call(
        body, "finish", [((showers, cells, width), BF16), ((steps, cells, width), F32)], [receive, scale], arrays,
        after=after, aliases={len(arrays) + 1: 0} if totals else None,
    )


def exclusive_prefix(parts):
    def body(p_ref, o_ref):
        total = jnp.zeros(parts.shape[1:], F32)
        for k in range(parts.shape[0]):
            o_ref[k] = total.astype(BF16)
            total = total + p_ref[k].astype(F32)

    return call(body, "exclusive_prefix", [(parts.shape, BF16)], [], [parts])[0]


def deliver(running, earlier):
    showers = len(running)
    steps, cells, width = running[0].shape
    every = [(step, shower) for step in range(steps) for shower in range(showers)]

    def body(*refs):
        run_refs, (early_ref, out_hbm, out_ref, sems) = refs[:showers], refs[showers:]
        stores = [
            pltpu.make_async_copy(out_ref.at[step, shower], out_hbm.at[step, shower], sems.at[i])
            for i, (step, shower) in enumerate(every)
        ]
        for i, (step, shower) in enumerate(every):
            out_ref[step, shower] = run_refs[shower][step] + early_ref[shower].astype(F32)
            stores[i].start()
        for store in stores:
            store.wait()

    shape = (steps, showers, cells, width)
    return call(
        body, "deliver", [], [], [*running, earlier], [], [(shape, F32)],
        scratch=[pltpu.VMEM(shape, F32), pltpu.SemaphoreType.DMA((len(every),))],
    )[0]


def local(
    iterates,
    noise_draws,
    drift_scale,
    noise_scale,
    step_embed,
    self_weight,
    neighbor_weight,
    output_weight,
    drift_weight,
    local_columns,
    tile_values,
    send_blocks,
    receive_rows,
    remote_values,
):
    steps, showers, cells, width = iterates.shape
    block = tile_values.shape[2]
    layers = self_weight.shape[0]
    parts = lax.axis_size("dom")
    pairs = [[(i, i ^ (1 << r)) for i in range(parts)] for r in range(2)]
    incoming = []
    for s in range(showers):
        sends = pack(iterates, s, send_blocks, block)
        incoming.append([lax.ppermute(sends[r], "dom", pairs[r]) for r in (0, 1)])
    common = (step_embed, self_weight, neighbor_weight, local_columns, tile_values)
    rest = (neighbor_weight, output_weight, remote_values, receive_rows)
    hidden, pre = [None] * showers, [None] * showers
    token = ()
    for s in range(showers):
        pre[s], hidden[s] = near_first(iterates, s, *common, token)
        token = (pre[s],)
    noise_sum = noise_sums(noise_draws, noise_scale, iterates, token)
    token = (noise_sum[0],)
    for layer in range(1, layers):
        for s in range(showers):
            hidden[s], *sends = far(hidden[s], incoming[s], pre[s], layer - 1, *rest, send_blocks, token)
            incoming[s] = [lax.ppermute(sends[r], "dom", pairs[r]) for r in (0, 1)]
            pre[s] = near(hidden[s], layer, *common, ())
            token = (pre[s],)
    totals, running = (), [None] * showers
    for s in range(showers):
        rounds = dict(enumerate(incoming[s]))
        if s > 0:
            pre[s] = middle(rounds.pop(0), pre[s], layers - 1, neighbor_weight, remote_values, receive_rows, totals)
        total, running[s] = finish(
            hidden[s], rounds, pre[s], layers - 1, s, showers, *rest, drift_weight, drift_scale, noise_sum[s],
            totals, token,
        )
        totals, token = (total,), ()
    pieces = lax.all_to_all(total.reshape(lax.axis_size("tm"), -1, width), "tm", 0, 0)
    earlier = lax.all_to_all(exclusive_prefix(pieces), "tm", 0, 0)
    return deliver(running, earlier.reshape(showers, cells, width))


def solution(mesh):
    return jax.shard_map(
        local,
        mesh=mesh,
        in_specs=(
            P("tm", None, "dom", None),
            P("tm", None, "dom", None),
            P("tm"),
            P("tm"),
            P("tm", None),
            P(),
            P(),
            P(),
            P(),
            P("dom", None),
            P("dom", None, None, None),
            P("dom", None, None),
            P("dom", None, None),
            P("dom", None, None, None, None),
        ),
        out_specs=P("tm", None, "dom", None),
        check_vma=False,
    )
```

```python
import jax
import jax.numpy as jnp
from jax import lax
from jax.experimental import pallas as pl
from jax.experimental.pallas import tpu as pltpu
from jax.sharding import PartitionSpec as P

F32 = jnp.float32
BF16 = jnp.bfloat16


def dot(a, b):
    return jnp.dot(a, b, preferred_element_type=F32)


def call(body, name, outs, scalars, arrays, far_arrays=(), far_outs=(), after=(), scratch=(), aliases=None):
    pin = lambda a: pltpu.with_memory_space_constraint(a, pltpu.VMEM)
    keep = lambda a: pltpu.with_memory_space_constraint(a, pltpu.HBM)
    count = len(scalars) + len(arrays) + len(far_arrays)
    vmem = pl.BlockSpec(memory_space=pltpu.VMEM)

    def inner(*refs):
        body(*refs[:count], *refs[count + len(after) :])

    return pl.pallas_call(
        inner,
        out_shape=[pltpu.VMEM(*o) for o in outs] + [pltpu.HBM(*o) for o in far_outs],
        in_specs=[pl.BlockSpec(memory_space=pltpu.SMEM)] * len(scalars)
        + [vmem] * len(arrays)
        + [pl.BlockSpec(memory_space=pltpu.HBM)] * len(far_arrays)
        + [vmem] * len(after),
        out_specs=[vmem] * len(outs) + [pl.BlockSpec(memory_space=pltpu.HBM)] * len(far_outs),
        scratch_shapes=list(scratch),
        input_output_aliases=aliases or {},
        compiler_params=pltpu.CompilerParams(vmem_limit_bytes=12 << 20),
        cost_estimate=pl.CostEstimate(flops=1 << 20, transcendentals=0, bytes_accessed=1 << 10),
        name=name,
    )(*scalars, *map(pin, arrays), *map(keep, far_arrays), *map(pin, after))


def pack(iterates, shower, send_blocks, block):
    steps, _, cells, width = iterates.shape
    rounds, sent = send_blocks.shape[1:]

    def body(blocks_hbm, it_hbm, *refs):
        send_refs, (blocks_ref, it_ref, sems) = refs[:rounds], refs[rounds:]
        index = pltpu.make_async_copy(blocks_hbm, blocks_ref, sems.at[steps])
        index.start()
        loads = [pltpu.make_async_copy(it_hbm.at[step, shower], it_ref.at[step], sems.at[step]) for step in range(steps)]
        for load in loads:
            load.start()
        index.wait()
        for step in range(steps):
            loads[step].wait()
            for r in range(rounds):
                for k in range(sent):
                    at = pl.ds(blocks_ref[0, r, k] * block, block)
                    send_refs[r][step, k] = it_ref[step, at, :].astype(BF16)

    return call(
        body, "pack", [((steps, sent, block, width), BF16)] * rounds, [], [], [send_blocks, iterates],
        scratch=[
            pltpu.SMEM(send_blocks.shape, jnp.int32), pltpu.VMEM((steps, cells, width), F32),
            pltpu.SemaphoreType.DMA((steps + 1,)),
        ],
    )


def near_step(col_ref, h_ref, emb_ref, ws, wn, tile_ref, pre_ref, step):
    parts, per_row, block, _ = tile_ref.shape
    mixed = []
    for b in range(parts):
        wide = jnp.concatenate([tile_ref[b, j] for j in range(per_row)], axis=1)
        tall = jnp.concatenate(
            [h_ref[step, pl.ds(col_ref[b, j] * block, block), :] for j in range(per_row)], axis=0
        )
        mixed.append(dot(wide, tall).astype(BF16))
    pre = dot(h_ref[step], ws) + dot(jnp.concatenate(mixed, axis=0), wn)
    pre_ref[step] = pre + emb_ref[step : step + 1, :]


def near(hidden, layer, embed, weight, neighbor, columns, tiles, after):
    steps, cells, width = hidden.shape

    def body(col_ref, h_ref, emb_ref, ws_ref, wn_ref, tile_ref, pre_ref):
        for step in range(steps):
            near_step(col_ref, h_ref, emb_ref, ws_ref[layer], wn_ref[layer], tile_ref, pre_ref, step)

    return call(
        body, "near", [((steps, cells, width), F32)], [columns], [hidden, embed, weight, neighbor, tiles], after=after
    )[0]


def near_first(iterates, shower, embed, weight, neighbor, columns, tiles, after):
    steps, _, cells, width = iterates.shape

    def body(col_ref, it_ref, emb_ref, ws_ref, wn_ref, tile_ref, pre_ref, h_ref):
        for step in range(steps):
            h_ref[step] = it_ref[step, shower].astype(BF16)
        for step in range(steps):
            near_step(col_ref, h_ref, emb_ref, ws_ref[0], wn_ref[0], tile_ref, pre_ref, step)

    return call(
        body, "near_first", [((steps, cells, width), F32), ((steps, cells, width), BF16)], [columns],
        [iterates, embed, weight, neighbor, tiles], after=after,
    )


def goes_to(recv_ref):
    return lambda r, k, b: jnp.where(recv_ref[0, r, k] == b, 1.0, 0.0)


def tables(receive, scale, parts, width, after):
    _, rounds, sent = receive.shape
    steps = scale.shape[0]

    def body(recv_ref, scale_ref, mask_ref, scales_ref):
        mask = goes_to(recv_ref)
        for i in range(rounds * sent * parts):
            r, k, b = i // (sent * parts), i // parts % sent, i % parts
            mask_ref[i] = jnp.broadcast_to(mask(r, k, b), (1, width))
        for step in range(steps):
            scales_ref[step] = jnp.broadcast_to(scale_ref[step], (1, width))

    outs = [((rounds * sent * parts, 1, width), F32), ((steps, 1, width), F32)]
    return call(body, "tables", outs, [receive, scale], [], after=after)


def received(mask, rem_ref, rounds, cells):
    steps, sent, block, _ = next(iter(rounds.values())).shape
    mixed = []
    for step in range(steps):
        addends = [((r, k), dot(rem_ref[0, r, k], in_ref[step, k])) for r, in_ref in rounds.items() for k in range(sent)]
        for b in range(cells // block):
            total = None
            for place, addend in addends:
                term = mask(*place, b) * addend
                total = term if total is None else total + term
            mixed.append(total.astype(BF16))
    return jnp.concatenate(mixed, axis=0)


def middle(incoming, pre, layer, neighbor, remote, receive, after):
    shape = pre.shape

    def body(recv_ref, in_ref, pre_ref, wn_ref, rem_ref, out_ref):
        mixed = received(goes_to(recv_ref), rem_ref, {0: in_ref}, shape[1])
        out_ref[...] = pre_ref[...] + dot(mixed, wn_ref[layer]).reshape(shape)

    return call(body, "middle", [(shape, F32)], [receive], [incoming, pre, neighbor, remote], after=after)[0]


def update(mask, h_ref, rounds, pre_ref, wn, wo, rem_ref):
    steps, cells, width = h_ref.shape
    half = 0.5 * (pre_ref[...].reshape(steps * cells, width) + dot(received(mask, rem_ref, rounds, cells), wn))
    activated = (half + half * jnp.tanh(half)).astype(BF16)
    before = h_ref[...].reshape(steps * cells, width).astype(F32)
    return (before + dot(activated, wo)).astype(BF16)


def far(hidden, incoming, pre, layer, neighbor, output, remote, receive, send_blocks, after):
    steps, cells, width = hidden.shape
    rounds, sent = send_blocks.shape[1:]
    block = incoming[0].shape[2]

    def body(recv_ref, blocks_ref, h_ref, *refs):
        in_refs, (pre_ref, wn_ref, wo_ref, rem_ref, out_ref, *send_refs) = refs[:rounds], refs[rounds:]
        rows = update(goes_to(recv_ref), h_ref, dict(enumerate(in_refs)), pre_ref, wn_ref[layer], wo_ref[layer], rem_ref)
        out_ref[...] = rows.reshape(steps, cells, width)
        for r in range(rounds):
            for k in range(sent):
                at = pl.ds(blocks_ref[0, r, k] * block, block)
                for step in range(steps):
                    send_refs[r][step, k] = out_ref[step, at, :]

    outs = [((steps, cells, width), BF16)] + [((steps, sent, block, width), BF16)] * rounds
    return call(
        body, "far", outs, [receive, send_blocks], [hidden, *incoming, pre, neighbor, output, remote], after=after
    )


def noise_sums(noise, scale, iterates, after):
    steps, showers, cells, width = noise.shape

    def body(scale_ref, nz_hbm, it_hbm, *refs):
        out_refs, (nz_ref, it_ref, sems) = refs[:showers], refs[showers:]
        loads = [pltpu.make_async_copy(it_hbm.at[0], it_ref, sems.at[0]), pltpu.make_async_copy(nz_hbm, nz_ref, sems.at[1])]
        for load in loads:
            load.start()
        for load in loads:
            load.wait()
        first = jnp.where(lax.axis_index("tm") == 0, 1.0, 0.0)
        for shower in range(showers):
            total = first * it_ref[shower]
            for step in range(steps):
                total = total + scale_ref[step] * nz_ref[step, shower].astype(F32)
                out_refs[shower][step] = total

    return call(
        body, "noise_sums", [((steps, cells, width), F32)] * showers, [scale], [], [noise, iterates], after=after,
        scratch=[
            pltpu.VMEM(noise.shape, BF16), pltpu.VMEM(iterates.shape[1:], F32), pltpu.SemaphoreType.DMA((2,)),
        ],
    )


def finish(hidden, incoming, pre, layer, shower, showers, neighbor, output, remote, drift_weight, vectors, noise_sum, totals, after):
    steps, cells, width = hidden.shape

    count = len(incoming)
    parts, sent = cells // remote.shape[3], remote.shape[2]

    def body(h_ref, *refs):
        rounds = dict(zip(incoming, refs[:count]))
        pre_ref, wn_ref, wo_ref, rem_ref, wd_ref, mask_ref, scale_ref, nz_ref, *_, tot_ref, run_ref = refs[count:]
        mask = lambda r, k, b: mask_ref[(r * sent + k) * parts + b]
        last = update(mask, h_ref, rounds, pre_ref, wn_ref[layer], wo_ref[layer], rem_ref)
        terms = dot(last, wd_ref[...])
        drift = None
        for step in range(steps):
            term = scale_ref[step] * terms[step * cells : (step + 1) * cells]
            drift = term if drift is None else drift + term
            run = drift + nz_ref[step]
            run_ref[step] = run
        tot_ref[shower] = run.astype(BF16)

    arrays = [hidden, *incoming.values(), pre, neighbor, output, remote, drift_weight, *vectors, noise_sum, *totals]
    return call(
        body, "finish", [((showers, cells, width), BF16), ((steps, cells, width), F32)], [], arrays,
        after=after, aliases={len(arrays) - 1: 0} if totals else None,
    )


def exclusive_prefix(parts):
    def body(p_ref, o_ref):
        total = jnp.zeros(parts.shape[1:], F32)
        for k in range(parts.shape[0]):
            o_ref[k] = total.astype(BF16)
            total = total + p_ref[k].astype(F32)

    return call(body, "exclusive_prefix", [(parts.shape, BF16)], [], [parts])[0]


def deliver(running, earlier):
    showers = len(running)
    steps, cells, width = running[0].shape
    every = [(step, shower) for step in range(steps) for shower in range(showers)]

    def body(*refs):
        run_refs, (early_ref, out_hbm, out_ref, sems) = refs[:showers], refs[showers:]
        stores = [
            pltpu.make_async_copy(out_ref.at[step, shower], out_hbm.at[step, shower], sems.at[i])
            for i, (step, shower) in enumerate(every)
        ]
        for i, (step, shower) in enumerate(every):
            out_ref[step, shower] = run_refs[shower][step] + early_ref[shower].astype(F32)
            stores[i].start()
        for store in stores:
            store.wait()

    shape = (steps, showers, cells, width)
    return call(
        body, "deliver", [], [], [*running, earlier], [], [(shape, F32)],
        scratch=[pltpu.VMEM(shape, F32), pltpu.SemaphoreType.DMA((len(every),))],
    )[0]


def local(
    iterates,
    noise_draws,
    drift_scale,
    noise_scale,
    step_embed,
    self_weight,
    neighbor_weight,
    output_weight,
    drift_weight,
    local_columns,
    tile_values,
    send_blocks,
    receive_rows,
    remote_values,
):
    steps, showers, cells, width = iterates.shape
    block = tile_values.shape[2]
    layers = self_weight.shape[0]
    parts = lax.axis_size("dom")
    pairs = [[(i, i ^ (1 << r)) for i in range(parts)] for r in range(2)]
    incoming = []
    for s in range(showers):
        sends = pack(iterates, s, send_blocks, block)
        incoming.append([lax.ppermute(sends[r], "dom", pairs[r]) for r in (0, 1)])
    common = (step_embed, self_weight, neighbor_weight, local_columns, tile_values)
    rest = (neighbor_weight, output_weight, remote_values, receive_rows)
    hidden, pre = [None] * showers, [None] * showers
    token = ()
    for s in range(showers):
        pre[s], hidden[s] = near_first(iterates, s, *common, token)
        token = (pre[s],)
    noise_sum = noise_sums(noise_draws, noise_scale, iterates, token)
    token = (noise_sum[0],)
    vectors = tables(receive_rows, drift_scale, cells // block, width, token)
    for layer in range(1, layers):
        for s in range(showers):
            hidden[s], *sends = far(hidden[s], incoming[s], pre[s], layer - 1, *rest, send_blocks, token)
            incoming[s] = [lax.ppermute(sends[r], "dom", pairs[r]) for r in (0, 1)]
            pre[s] = near(hidden[s], layer, *common, ())
            token = (pre[s],)
    totals, running = (), [None] * showers
    for s in range(showers):
        rounds = dict(enumerate(incoming[s]))
        if s > 0:
            pre[s] = middle(rounds.pop(0), pre[s], layers - 1, neighbor_weight, remote_values, receive_rows, totals)
        total, running[s] = finish(
            hidden[s], rounds, pre[s], layers - 1, s, showers, *rest[:3], drift_weight, vectors, noise_sum[s],
            totals, token,
        )
        totals, token = (total,), ()
    pieces = lax.all_to_all(total.reshape(lax.axis_size("tm"), -1, width), "tm", 0, 0)
    earlier = lax.all_to_all(exclusive_prefix(pieces), "tm", 0, 0)
    return deliver(running, earlier.reshape(showers, cells, width))


def solution(mesh):
    return jax.shard_map(
        local,
        mesh=mesh,
        in_specs=(
            P("tm", None, "dom", None),
            P("tm", None, "dom", None),
            P("tm"),
            P("tm"),
            P("tm", None),
            P(),
            P(),
            P(),
            P(),
            P("dom", None),
            P("dom", None, None, None),
            P("dom", None, None),
            P("dom", None, None),
            P("dom", None, None, None, None),
        ),
        out_specs=P("tm", None, "dom", None),
        check_vma=False,
    )
```

```python
import jax
import jax.numpy as jnp
from jax import lax
from jax.experimental import pallas as pl
from jax.experimental.pallas import tpu as pltpu
from jax.sharding import PartitionSpec as P

F32 = jnp.float32
BF16 = jnp.bfloat16


def dot(a, b):
    return jnp.dot(a, b, preferred_element_type=F32)


def call(body, name, outs, scalars, arrays, far_arrays=(), far_outs=(), after=(), scratch=(), aliases=None):
    pin = lambda a: pltpu.with_memory_space_constraint(a, pltpu.VMEM)
    keep = lambda a: pltpu.with_memory_space_constraint(a, pltpu.HBM)
    count = len(scalars) + len(arrays) + len(far_arrays)
    vmem = pl.BlockSpec(memory_space=pltpu.VMEM)

    def inner(*refs):
        body(*refs[:count], *refs[count + len(after) :])

    return pl.pallas_call(
        inner,
        out_shape=[pltpu.VMEM(*o) for o in outs] + [pltpu.HBM(*o) for o in far_outs],
        in_specs=[pl.BlockSpec(memory_space=pltpu.SMEM)] * len(scalars)
        + [vmem] * len(arrays)
        + [pl.BlockSpec(memory_space=pltpu.HBM)] * len(far_arrays)
        + [vmem] * len(after),
        out_specs=[vmem] * len(outs) + [pl.BlockSpec(memory_space=pltpu.HBM)] * len(far_outs),
        scratch_shapes=list(scratch),
        input_output_aliases=aliases or {},
        compiler_params=pltpu.CompilerParams(vmem_limit_bytes=12 << 20),
        cost_estimate=pl.CostEstimate(flops=1 << 20, transcendentals=0, bytes_accessed=1 << 10),
        name=name,
    )(*scalars, *map(pin, arrays), *map(keep, far_arrays), *map(pin, after))


def pack(iterates, shower, send_blocks, block):
    steps, _, cells, width = iterates.shape
    rounds, sent = send_blocks.shape[1:]

    def body(blocks_hbm, it_hbm, *refs):
        send_refs, (blocks_ref, it_ref, sems) = refs[:rounds], refs[rounds:]
        index = pltpu.make_async_copy(blocks_hbm, blocks_ref, sems.at[steps])
        index.start()
        loads = [pltpu.make_async_copy(it_hbm.at[step, shower], it_ref.at[step], sems.at[step]) for step in range(steps)]
        for load in loads:
            load.start()
        index.wait()
        for step in range(steps):
            loads[step].wait()
            for r in range(rounds):
                for k in range(sent):
                    at = pl.ds(blocks_ref[0, r, k] * block, block)
                    send_refs[r][step, k] = it_ref[step, at, :].astype(BF16)

    return call(
        body, "pack", [((steps, sent, block, width), BF16)] * rounds, [], [], [send_blocks, iterates],
        scratch=[
            pltpu.SMEM(send_blocks.shape, jnp.int32), pltpu.VMEM((steps, cells, width), F32),
            pltpu.SemaphoreType.DMA((steps + 1,)),
        ],
    )


def near_step(col_ref, h_ref, emb_ref, ws, wn, tile_ref, pre_ref, step):
    parts, per_row, block, _ = tile_ref.shape
    mixed = []
    for b in range(parts):
        wide = jnp.concatenate([tile_ref[b, j] for j in range(per_row)], axis=1)
        tall = jnp.concatenate(
            [h_ref[step, pl.ds(col_ref[b, j] * block, block), :] for j in range(per_row)], axis=0
        )
        mixed.append(dot(wide, tall).astype(BF16))
    pre = dot(h_ref[step], ws) + dot(jnp.concatenate(mixed, axis=0), wn)
    pre_ref[step] = pre + emb_ref[step : step + 1, :]


def near(hidden, layer, embed, weight, neighbor, columns, tiles, after):
    steps, cells, width = hidden.shape

    def body(col_ref, h_ref, emb_ref, ws_ref, wn_ref, tile_ref, pre_ref):
        for step in range(steps):
            near_step(col_ref, h_ref, emb_ref, ws_ref[layer], wn_ref[layer], tile_ref, pre_ref, step)

    return call(
        body, "near", [((steps, cells, width), F32)], [columns], [hidden, embed, weight, neighbor, tiles], after=after
    )[0]


def near_first(iterates, shower, embed, weight, neighbor, columns, tiles, after):
    steps, _, cells, width = iterates.shape

    def body(col_ref, it_ref, emb_ref, ws_ref, wn_ref, tile_ref, pre_ref, h_ref):
        for step in range(steps):
            h_ref[step] = it_ref[step, shower].astype(BF16)
        for step in range(steps):
            near_step(col_ref, h_ref, emb_ref, ws_ref[0], wn_ref[0], tile_ref, pre_ref, step)

    return call(
        body, "near_first", [((steps, cells, width), F32), ((steps, cells, width), BF16)], [columns],
        [iterates, embed, weight, neighbor, tiles], after=after,
    )


def goes_to(recv_ref):
    return lambda r, k, b: jnp.where(recv_ref[0, r, k] == b, 1.0, 0.0)


def tables(receive, scale, parts, width, after):
    _, rounds, sent = receive.shape
    steps = scale.shape[0]

    def body(recv_ref, scale_ref, mask_ref, scales_ref):
        mask = goes_to(recv_ref)
        for i in range(rounds * sent * parts):
            r, k, b = i // (sent * parts), i // parts % sent, i % parts
            mask_ref[i] = jnp.broadcast_to(mask(r, k, b), (1, width))
        for step in range(steps):
            scales_ref[step] = jnp.broadcast_to(scale_ref[step], (1, width))

    outs = [((rounds * sent * parts, 1, width), F32), ((steps, 1, width), F32)]
    return call(body, "tables", outs, [receive, scale], [], after=after)


def received(mask, rem_ref, rounds, cells):
    steps, sent, block, _ = next(iter(rounds.values())).shape
    mixed = []
    for step in range(steps):
        addends = [((r, k), dot(rem_ref[0, r, k], in_ref[step, k])) for r, in_ref in rounds.items() for k in range(sent)]
        for b in range(cells // block):
            total = None
            for place, addend in addends:
                term = mask(*place, b) * addend
                total = term if total is None else total + term
            mixed.append(total.astype(BF16))
    return jnp.concatenate(mixed, axis=0)


def middle(incoming, pre, layer, neighbor, remote, receive, after):
    shape = pre.shape

    def body(recv_ref, in_ref, pre_ref, wn_ref, rem_ref, out_ref):
        mixed = received(goes_to(recv_ref), rem_ref, {0: in_ref}, shape[1])
        out_ref[...] = pre_ref[...] + dot(mixed, wn_ref[layer]).reshape(shape)

    return call(body, "middle", [(shape, F32)], [receive], [incoming, pre, neighbor, remote], after=after)[0]


def update(mask, h_ref, rounds, pre_ref, wn, wo, rem_ref):
    steps, cells, width = h_ref.shape
    half = 0.5 * (pre_ref[...].reshape(steps * cells, width) + dot(received(mask, rem_ref, rounds, cells), wn))
    activated = (half + half * jnp.tanh(half)).astype(BF16)
    before = h_ref[...].reshape(steps * cells, width).astype(F32)
    return (before + dot(activated, wo)).astype(BF16)


def far(hidden, incoming, pre, layer, neighbor, output, remote, receive, send_blocks, after):
    steps, cells, width = hidden.shape
    rounds, sent = send_blocks.shape[1:]
    block = incoming[0].shape[2]

    def body(recv_ref, blocks_ref, h_ref, *refs):
        in_refs, (pre_ref, wn_ref, wo_ref, rem_ref, out_ref, *send_refs) = refs[:rounds], refs[rounds:]
        rows = update(goes_to(recv_ref), h_ref, dict(zip(incoming, in_refs)), pre_ref, wn_ref[layer], wo_ref[layer], rem_ref)
        out_ref[...] = rows.reshape(steps, cells, width)
        for r in range(rounds):
            for k in range(sent):
                at = pl.ds(blocks_ref[0, r, k] * block, block)
                for step in range(steps):
                    send_refs[r][step, k] = out_ref[step, at, :]

    outs = [((steps, cells, width), BF16)] + [((steps, sent, block, width), BF16)] * rounds
    return call(
        body, "far", outs, [receive, send_blocks], [hidden, *incoming.values(), pre, neighbor, output, remote], after=after
    )


def noise_sums(noise, scale, iterates, after):
    steps, showers, cells, width = noise.shape

    def body(scale_ref, nz_hbm, it_hbm, *refs):
        out_refs, (nz_ref, it_ref, sems) = refs[:showers], refs[showers:]
        loads = [pltpu.make_async_copy(it_hbm.at[0], it_ref, sems.at[0]), pltpu.make_async_copy(nz_hbm, nz_ref, sems.at[1])]
        for load in loads:
            load.start()
        for load in loads:
            load.wait()
        first = jnp.where(lax.axis_index("tm") == 0, 1.0, 0.0)
        for shower in range(showers):
            total = first * it_ref[shower]
            for step in range(steps):
                total = total + scale_ref[step] * nz_ref[step, shower].astype(F32)
                out_refs[shower][step] = total

    return call(
        body, "noise_sums", [((steps, cells, width), F32)] * showers, [scale], [], [noise, iterates], after=after,
        scratch=[
            pltpu.VMEM(noise.shape, BF16), pltpu.VMEM(iterates.shape[1:], F32), pltpu.SemaphoreType.DMA((2,)),
        ],
    )


def finish(hidden, incoming, pre, layer, shower, showers, neighbor, output, remote, drift_weight, vectors, noise_sum, totals, after):
    steps, cells, width = hidden.shape

    count = len(incoming)
    parts, sent = cells // remote.shape[3], remote.shape[2]

    def body(h_ref, *refs):
        rounds = dict(zip(incoming, refs[:count]))
        pre_ref, wn_ref, wo_ref, rem_ref, wd_ref, mask_ref, scale_ref, nz_ref, *_, tot_ref, run_ref = refs[count:]
        mask = lambda r, k, b: mask_ref[(r * sent + k) * parts + b]
        last = update(mask, h_ref, rounds, pre_ref, wn_ref[layer], wo_ref[layer], rem_ref)
        terms = dot(last, wd_ref[...])
        drift = None
        for step in range(steps):
            term = scale_ref[step] * terms[step * cells : (step + 1) * cells]
            drift = term if drift is None else drift + term
            run = drift + nz_ref[step]
            run_ref[step] = run
        tot_ref[shower] = run.astype(BF16)

    arrays = [hidden, *incoming.values(), pre, neighbor, output, remote, drift_weight, *vectors, noise_sum, *totals]
    return call(
        body, "finish", [((showers, cells, width), BF16), ((steps, cells, width), F32)], [], arrays,
        after=after, aliases={len(arrays) - 1: 0} if totals else None,
    )


def exclusive_prefix(parts):
    def body(p_ref, o_ref):
        total = jnp.zeros(parts.shape[1:], F32)
        for k in range(parts.shape[0]):
            o_ref[k] = total.astype(BF16)
            total = total + p_ref[k].astype(F32)

    return call(body, "exclusive_prefix", [(parts.shape, BF16)], [], [parts])[0]


def deliver(running, earlier):
    showers = len(running)
    steps, cells, width = running[0].shape
    every = [(step, shower) for step in range(steps) for shower in range(showers)]

    def body(*refs):
        run_refs, (early_ref, out_hbm, out_ref, sems) = refs[:showers], refs[showers:]
        stores = [
            pltpu.make_async_copy(out_ref.at[step, shower], out_hbm.at[step, shower], sems.at[i])
            for i, (step, shower) in enumerate(every)
        ]
        for i, (step, shower) in enumerate(every):
            out_ref[step, shower] = run_refs[shower][step] + early_ref[shower].astype(F32)
            stores[i].start()
        for store in stores:
            store.wait()

    shape = (steps, showers, cells, width)
    return call(
        body, "deliver", [], [], [*running, earlier], [], [(shape, F32)],
        scratch=[pltpu.VMEM(shape, F32), pltpu.SemaphoreType.DMA((len(every),))],
    )[0]


def local(
    iterates,
    noise_draws,
    drift_scale,
    noise_scale,
    step_embed,
    self_weight,
    neighbor_weight,
    output_weight,
    drift_weight,
    local_columns,
    tile_values,
    send_blocks,
    receive_rows,
    remote_values,
):
    steps, showers, cells, width = iterates.shape
    block = tile_values.shape[2]
    layers = self_weight.shape[0]
    parts = lax.axis_size("dom")
    pairs = [[(i, i ^ (1 << r)) for i in range(parts)] for r in range(2)]
    incoming = []
    for s in range(showers):
        sends = pack(iterates, s, send_blocks, block)
        incoming.append({r: lax.ppermute(sends[r], "dom", pairs[r]) for r in (1, 0)})
    common = (step_embed, self_weight, neighbor_weight, local_columns, tile_values)
    rest = (neighbor_weight, output_weight, remote_values, receive_rows)
    hidden, pre = [None] * showers, [None] * showers
    token = ()
    for s in range(showers):
        pre[s], hidden[s] = near_first(iterates, s, *common, token)
        token = (pre[s],)
    noise_sum = noise_sums(noise_draws, noise_scale, iterates, token)
    token = (noise_sum[0],)
    vectors = tables(receive_rows, drift_scale, cells // block, width, token)
    for layer in range(1, layers):
        for s in range(showers):
            hidden[s], *sends = far(hidden[s], incoming[s], pre[s], layer - 1, *rest, send_blocks, token)
            incoming[s] = {r: lax.ppermute(sends[r], "dom", pairs[r]) for r in (1, 0)}
            pre[s] = near(hidden[s], layer, *common, ())
            token = (pre[s],)
    totals, running = (), [None] * showers
    for s in range(showers):
        rounds = dict(incoming[s])
        if s > 0:
            pre[s] = middle(rounds.pop(0), pre[s], layers - 1, neighbor_weight, remote_values, receive_rows, totals)
        total, running[s] = finish(
            hidden[s], rounds, pre[s], layers - 1, s, showers, *rest[:3], drift_weight, vectors, noise_sum[s],
            totals, token,
        )
        totals, token = (total,), ()
    pieces = lax.all_to_all(total.reshape(lax.axis_size("tm"), -1, width), "tm", 0, 0)
    earlier = lax.all_to_all(exclusive_prefix(pieces), "tm", 0, 0)
    return deliver(running, earlier.reshape(showers, cells, width))


def solution(mesh):
    return jax.shard_map(
        local,
        mesh=mesh,
        in_specs=(
            P("tm", None, "dom", None),
            P("tm", None, "dom", None),
            P("tm"),
            P("tm"),
            P("tm", None),
            P(),
            P(),
            P(),
            P(),
            P("dom", None),
            P("dom", None, None, None),
            P("dom", None, None),
            P("dom", None, None),
            P("dom", None, None, None, None),
        ),
        out_specs=P("tm", None, "dom", None),
        check_vma=False,
    )
```
